128 devices in a mesh: row: 16 (over y, z), col: 8 (over x, core).
Axes of the slice: x: 4, y: 4, z: 4, core: 2. Of those that a mesh axis runs over, the one named last changes fastest.
Arguments:
- vectors: bfloat16 [12288, 256, 64], P(('row', 'col')), may hold values from -6 to 6
- energies: float32 [12288, 256], P(('row', 'col')), may hold values from 1 to 3
- blocks: bfloat16 [12288, 256, 256], P(('row', 'col')), may hold values from -0.375 to 0.375
- kernel: bfloat16 [16384, 16384], P('row', 'col'), may hold values from -0.00390625 to 0.00390625
- slot_coarse_kpoint: int32 [12288], P(('row', 'col')), may hold values from 0 to 63
- counts: int32 [128], P(('row', 'col')), may hold values from 1 to 96, 8192 in all
Outputs:
- filtered: bfloat16 [12288, 256, 64], P(('row', 'col'))
The draws below stay inside these ranges and needn't reach their ends.
Inputs may be any that keep to these rules, and one draw needn't show every extreme that they name: Device d (index row * 8 + col in mesh order) holds live fine k-points in its first counts[d] slots; one device has exactly 96.
All inputs are finite; a program needn't handle non-finite values.
Results may differ from the reference program's by a relative error of at most 0.009.
Values may be sent and summed in bfloat16 or wider, within the bound.
A program may use at most 128 MiB of HBM per device.

```python
import math
import jax
import jax.numpy as jnp
import numpy as np
from jax import lax

KPOINT_TRANSITNS = 256
FILTER_VECTORS = 64
CORDER = 16384
SLOTS = 96
COARSE_KPOINTS = 64
FINE_SLOT_TOTAL = 12288
FINE = 8192
DEVICES = 128


def set_ends(array, rng, low, top_value):
    longest = array.shape.index(max(array.shape))
    spots = []
    for shift in (0, 1):
        where = [jax.random.randint(jax.random.fold_in(rng, axis), (), 0, length) for axis, length in enumerate(array.shape)]
        where[longest] = (where[longest] + shift) % array.shape[longest]
        spots.append(tuple(where))
    return array.at[spots[0]].set(low).at[spots[1]].set(top_value)


def steps_of(own_key, shape, pieces, least, high):
    loudness, own = 1.0, jax.random.fold_in(own_key, 6)
    for dim, parts in pieces:
        steps = jnp.exp(jax.random.uniform(jax.random.fold_in(own, dim), (parts,), jnp.float32, least / len(pieces), high / len(pieces)))
        loudness = loudness * jnp.repeat(steps, shape[dim] // parts).reshape([-1 if axis == dim else 1 for axis in range(len(shape))])
    return loudness


def length_profile(count, total, most, skew):
    weights = [(1 << 20) // math.isqrt(rank ** skew) + 1 for rank in range(2, count + 1)]
    spare, holding = total - most - (count - 1), [1] * (count - 1)
    while spare > 0:
        free = [i for i in range(count - 1) if holding[i] < most]
        whole, left = sum([weights[i] for i in free]), spare
        for i in free:
            addition = min(most - holding[i], max(1, left * weights[i] // whole), spare)
            holding[i] = holding[i] + addition
            spare = spare - addition
    return np.array([most] + holding)


def ragged(own_key, amount, total, reach, slope):
    if amount == 2:
        one = jax.random.randint(own_key, (), max(1, total - reach), min(reach, total - 1) + 1)
        return jnp.stack([one, total - one])
    sizes = jnp.asarray(length_profile(amount, total, reach, slope), jnp.int32)
    couples = (amount - 1) // 2
    source_of, sink = sizes[1:1 + 2 * couples:2], sizes[2:2 + 2 * couples:2]
    slack = jnp.minimum(source_of - 1, reach - sink)
    moved = jax.random.randint(jax.random.fold_in(own_key, 1), (couples,), 0, 1 << 20) % (slack + 1)
    sizes = sizes.at[1:1 + 2 * couples:2].set(source_of - moved).at[2:2 + 2 * couples:2].set(sink + moved)
    return sizes[jax.random.permutation(jax.random.fold_in(own_key, 2), amount)]


def bell_draw(rng, extent, scale, reach, split=(), kind=jnp.bfloat16):
    array = jax.random.normal(rng, extent, jnp.float32) * scale
    if len(split) > 0:
        array = steps_of(rng, extent, split, -0.22, 0.18) * array
    return jnp.clip(array, min=-reach, max=reach).astype(kind)


def setup_inputs(seed: int = 0) -> dict:
    splits = jax.random.split(jax.random.key(seed), 7)
    return {
        "vectors": bell_draw(splits[0], (FINE_SLOT_TOTAL, KPOINT_TRANSITNS, FILTER_VECTORS), 1.0, 6.0, ((0, 128),)),
        "energies": jnp.clip(1.0 + 2.0 * jax.random.uniform(splits[1], (FINE_SLOT_TOTAL, KPOINT_TRANSITNS), jnp.float32) ** steps_of(splits[1], (FINE_SLOT_TOTAL, KPOINT_TRANSITNS), ((0, 128),), -0.2, 0.2), 1.0, 3.0),
        "blocks": bell_draw(splits[2], (FINE_SLOT_TOTAL, KPOINT_TRANSITNS, KPOINT_TRANSITNS), KPOINT_TRANSITNS ** -0.5, 0.375, ((0, 128),)),
        "kernel": bell_draw(splits[3], (CORDER, CORDER), (CORDER * 128) ** -0.5, 0.00390625, ((0, 16), (1, 8))),
        "slot_coarse_kpoint": set_ends(jax.random.randint(splits[4], (FINE_SLOT_TOTAL,), 0, COARSE_KPOINTS), jax.random.fold_in(splits[4], 1), 0, COARSE_KPOINTS - 1).astype(jnp.int32),
        "counts": ragged(splits[5], DEVICES, FINE, SLOTS, 2).astype(jnp.int32),
    }


def forward_blocks(blocks, xb):
    def unit_factor(pair):
        mats, vecs = pair
        return jnp.einsum("sij,sjv->siv", mats.astype(jnp.float32), vecs.astype(jnp.float32), precision=lax.Precision.HIGHEST)
    reshaped_block = blocks.reshape(DEVICES, SLOTS, KPOINT_TRANSITNS, KPOINT_TRANSITNS)
    vector_reshaped = xb.reshape(DEVICES, SLOTS, KPOINT_TRANSITNS, FILTER_VECTORS)
    return lax.map(unit_factor, (reshaped_block, vector_reshaped)).reshape(FINE_SLOT_TOTAL, KPOINT_TRANSITNS, FILTER_VECTORS)


def backward_blocks(blocks, picked):
    def unit_factor(pair):
        mats, vecs = pair
        return jnp.einsum("sji,sjv->siv", mats.astype(jnp.float32), vecs.astype(jnp.float32), precision=lax.Precision.HIGHEST)
    reshaped_block = blocks.reshape(DEVICES, SLOTS, KPOINT_TRANSITNS, KPOINT_TRANSITNS)
    vector_reshaped = picked.reshape(DEVICES, SLOTS, KPOINT_TRANSITNS, FILTER_VECTORS)
    return lax.map(unit_factor, (reshaped_block, vector_reshaped)).reshape(FINE_SLOT_TOTAL, KPOINT_TRANSITNS, FILTER_VECTORS)


def apply_hamiltonian(xb, energies, blocks, kernel, slot_coarse_kpoint, live):
    proj = forward_blocks(blocks, xb)
    summed = jax.ops.segment_sum(proj, slot_coarse_kpoint, num_segments=COARSE_KPOINTS)
    ubf = summed.reshape(CORDER, FILTER_VECTORS).astype(jnp.bfloat16)
    wbf = jnp.dot(kernel, ubf, preferred_element_type=jnp.float32).astype(jnp.bfloat16)
    picked = wbf.reshape(COARSE_KPOINTS, KPOINT_TRANSITNS, FILTER_VECTORS)[slot_coarse_kpoint]
    back = backward_blocks(blocks, picked)
    return energies[:, :, None] * xb.astype(jnp.float32) + live[:, None, None] * back


def reference(vectors, energies, blocks, kernel, slot_coarse_kpoint, counts):
    slot_index_list = jnp.arange(FINE_SLOT_TOTAL, dtype=jnp.int32)
    owners = slot_index_list // SLOTS
    live = ((slot_index_list % SLOTS) < counts[owners]).astype(jnp.float32)
    start = live[:, None, None] * vectors.astype(jnp.float32)
    startb = start.astype(jnp.bfloat16)
    first = (apply_hamiltonian(startb, energies, blocks, kernel, slot_coarse_kpoint, live) - 2.0 * start) / 2.0
    firstb = first.astype(jnp.bfloat16)
    second = apply_hamiltonian(firstb, energies, blocks, kernel, slot_coarse_kpoint, live)
    result = 2.0 * (second - 2.0 * firstb.astype(jnp.float32)) / 2.0 - start
    return result.astype(jnp.bfloat16)
```

```python
import functools

import jax
import jax.numpy as jnp
from jax import lax
from jax.experimental import pallas as pl
from jax.experimental.pallas import tpu as pltpu
from jax.sharding import PartitionSpec as P

MESH = pl.DeviceIdType.MESH
F32 = jnp.float32
BF16 = jnp.bfloat16
STEP = 8
X, Y, Z = 0, 1, 2
ORDERS = ((X, Y, Z), (Y, Z, X), (Z, X, Y), (X, Z, Y))
NT = (((1,), (1,)), ((), ()))


def position():
    r, c = lax.axis_index("row"), lax.axis_index("col")
    return (c // 2, r // 4, r % 4, c % 2)


def device(x, y, z, k):
    return (y * 4 + z, x * 2 + k)


def peer(here, dim, step):
    there = list(here)
    there[dim] = (there[dim] + step) % 4
    return device(*there)


def at_dim(dim, index, rank):
    return tuple(index if d == dim else slice(None) for d in range(rank))


def coarse_body(u_ref, k_hbm, w_ref, kv, core_in, s1, r1, s2, r2, s3, r3, ub, ul, pw, rw,
                k_sem, core_ss, core_rs, rs_ss, rs_rs, yz_ss, yz_rs, pr_ss, pr_rs, ag_ss, ag_rs, fin_ss, fin_rs):
    here = position()
    x, y, z, k = here
    me = (y * 4 + z) * 8 + x * 2 + k
    sibling = device(x, y, z, 1 - k)
    yz_steps = [(i // 4, i % 4) for i in range(1, 16)]
    yz_peers = [device(x, (y + a) % 4, (z + b) % 4, k) for a, b in yz_steps]
    xk_steps = [(i // 2, i % 2) for i in range(1, 8)]
    xk_peers = [device((x + a) % 4, y, z, (k + b) % 2) for a, b in xk_steps]

    load = pltpu.make_async_copy(k_hbm, kv, k_sem)
    load.start()

    barrier = pltpu.get_barrier_semaphore()
    for p in yz_peers + xk_peers:
        pl.semaphore_signal(barrier, inc=1, device_id=p, device_id_type=MESH)
    pl.semaphore_wait(barrier, 22)

    def send(src, dst, ss, rs, to):
        copy = pltpu.make_async_remote_copy(src_ref=src, dst_ref=dst, send_sem=ss, recv_sem=rs, device_id=to, device_id_type=MESH)
        copy.start()
        return copy

    waits = []
    core = [send(u_ref.at[:, 1 - k, :, :, g], core_in.at[g], core_ss.at[g], core_rs.at[g], sibling) for g in range(4)]
    first = []
    for g in range(4):
        core[g].wait_recv()
        for a in range(4):
            s1[g, a] = (u_ref[a, k, :, :, g].astype(F32) + core_in[g, a].astype(F32)).astype(BF16)
        d = ORDERS[g][0]
        first.append([send(s1.at[(g,) + at_dim(d, (here[d] + o) % 4, 3)], r1.at[g, o - 1], rs_ss.at[g, 0, o - 1], rs_rs.at[g, 0, o - 1], peer(here, d, o)) for o in (1, 2, 3)])
    second = []
    for g in range(4):
        d, e, f = ORDERS[g]
        for c in first[g]:
            c.wait_recv()
        own = s1[(g,) + at_dim(d, here[d], 3)]
        s2[g] = (own.astype(F32) + r1[g, 0].astype(F32) + r1[g, 1].astype(F32) + r1[g, 2].astype(F32)).astype(BF16)
        at = 0 if e < f else 1
        second.append([send(s2.at[(g,) + at_dim(at, (here[e] + o) % 4, 2)], r2.at[g, o - 1], rs_ss.at[g, 1, o - 1], rs_rs.at[g, 1, o - 1], peer(here, e, o)) for o in (1, 2, 3)])
    third = []
    for g in range(4):
        d, e, f = ORDERS[g]
        for c in second[g]:
            c.wait_recv()
        at = 0 if e < f else 1
        own = s2[(g,) + at_dim(at, here[e], 2)]
        s3[g] = (own.astype(F32) + r2[g, 0].astype(F32) + r2[g, 1].astype(F32) + r2[g, 2].astype(F32)).astype(BF16)
        third.append([send(s3.at[g, (here[f] + o) % 4], r3.at[g, o - 1], rs_ss.at[g, 2, o - 1], rs_rs.at[g, 2, o - 1], peer(here, f, o)) for o in (1, 2, 3)])
    for g in range(4):
        f = ORDERS[g][2]
        for c in third[g]:
            c.wait_recv()
        total = s3[g, here[f]].astype(F32) + r3[g, 0].astype(F32) + r3[g, 1].astype(F32) + r3[g, 2].astype(F32)
        ub[y, z, g] = total.astype(BF16)
    spread = [send(ub.at[y, z], ub.at[y, z], yz_ss.at[i], yz_rs.at[i], yz_peers[i]) for i in range(15)]
    for c in core:
        c.wait_send()
    for c in sum(first + second + third, []):
        c.wait_send()
    load.wait()
    for c in spread:
        c.wait()
    for q in range(16):
        for g in range(4):
            ul[g * 16 : g * 16 + 16, q * 128 : q * 128 + 128] = ub[q // 4, q % 4, g]
    for n in range(4):
        part = lax.dot_general(ul[...], kv[n * 256 : n * 256 + 256, :], NT, preferred_element_type=F32).astype(BF16)
        for h in range(2):
            for g in range(4):
                pw[n, h, g] = part[g * 16 : g * 16 + 16, h * 128 : h * 128 + 128]
    swap = [send(pw.at[(x + a) % 4, (k + b) % 2], rw.at[i], pr_ss.at[i], pr_rs.at[i], xk_peers[i]) for i, (a, b) in enumerate(xk_steps)]
    for c in swap:
        c.wait()
    total = pw[x, k].astype(F32)
    for i in range(7):
        total = total + rw[i].astype(F32)
    w_ref[y, z, x, k] = total.astype(BF16)

    def part_of(g, free):
        ix = [slice(None) if d in free else here[d] for d in range(3)]
        return w_ref.at[ix[1], ix[2], ix[0], k, g]

    stages = []
    for stage in range(3):
        now = []
        for g in range(4):
            order = ORDERS[g][::-1]
            if stage > 0:
                for c in stages[stage - 1][g]:
                    c.wait_recv()
            block = part_of(g, order[:stage])
            now.append([send(block, block, ag_ss.at[g, stage, o - 1], ag_rs.at[g, stage, o - 1], peer(here, order[stage], o)) for o in (1, 2, 3)])
        stages.append(now)
    last = []
    for g in range(4):
        for c in stages[2][g]:
            c.wait_recv()
        block = part_of(g, (X, Y, Z))
        last.append(send(block, block, fin_ss.at[g], fin_rs.at[g], sibling))
    for now in stages:
        for c in sum(now, []):
            c.wait_send()
    for c in last:
        c.wait()


def coarse(part, kernel):
    dma = pltpu.SemaphoreType.DMA
    whole = pl.pallas_call(
        coarse_body,
        name="coarse",
        out_shape=jax.ShapeDtypeStruct((4, 4, 4, 2, 4, 16, 128), BF16),
        in_specs=[pl.BlockSpec(memory_space=pltpu.VMEM), pl.BlockSpec(memory_space=pl.ANY)],
        out_specs=pl.BlockSpec(memory_space=pltpu.VMEM),
        scratch_shapes=[
            pltpu.VMEM(kernel.shape, BF16),
            pltpu.VMEM((4, 4, 4, 4, 16, 128), BF16),
            pltpu.VMEM((4, 4, 4, 4, 16, 128), BF16),
            pltpu.VMEM((4, 3, 4, 4, 16, 128), BF16),
            pltpu.VMEM((4, 4, 4, 16, 128), BF16),
            pltpu.VMEM((4, 3, 4, 16, 128), BF16),
            pltpu.VMEM((4, 4, 16, 128), BF16),
            pltpu.VMEM((4, 3, 16, 128), BF16),
            pltpu.VMEM((4, 4, 4, 16, 128), BF16),
            pltpu.VMEM((64, 2048), BF16),
            pltpu.VMEM((4, 2, 4, 16, 128), BF16),
            pltpu.VMEM((7, 4, 16, 128), BF16),
            dma, dma((4,)), dma((4,)), dma((4, 3, 3)), dma((4, 3, 3)), dma((15,)), dma((15,)), dma((7,)), dma((7,)),
            dma((4, 3, 3)), dma((4, 3, 3)), dma((4,)), dma((4,)),
        ],
        compiler_params=pltpu.CompilerParams(collective_id=0, has_side_effects=True, vmem_limit_bytes=40 << 20),
    )(part.reshape(4, 2, 4, 4, 4, 16, 128), kernel)
    return whole.reshape(64, 2, 64, 128)


def add_in(acc, points, slot, value):
    p = points[slot]
    acc[p, 0] += value[:, :128]
    acc[p, 1] += value[:, 128:]


def project_body(points, counts, v_ref, b_ref, u_ref, acc):
    step = pl.program_id(0)

    @pl.when(step == 0)
    def _():
        acc[...] = jnp.zeros_like(acc)

    for s in range(STEP):
        slot = step * STEP + s
        live = (slot < counts[0]).astype(BF16)
        value = lax.dot_general(v_ref[s] * live, b_ref[s], NT, preferred_element_type=F32)
        add_in(acc, points, slot, value)

    @pl.when(step == pl.num_programs(0) - 1)
    def _():
        u_ref[...] = acc[...].astype(BF16)


def back_of(points, slot, w_ref, b):
    p = points[slot]
    w = jnp.concatenate([w_ref[p, 0], w_ref[p, 1]], axis=1)
    return jnp.dot(w, b, preferred_element_type=F32)


def middle_body(points, counts, v_ref, e_ref, b_ref, w_ref, t_ref, u_ref, acc):
    step = pl.program_id(0)

    @pl.when(step == 0)
    def _():
        acc[...] = jnp.zeros_like(acc)

    for s in range(STEP):
        slot = step * STEP + s
        live = (slot < counts[0]).astype(F32)
        back = back_of(points, slot, w_ref, b_ref[s])
        start = v_ref[s].astype(F32)
        first = (((e_ref[s : s + 1] - 2.0) * start + back) * (0.5 * live)).astype(BF16)
        t_ref[s] = first
        value = lax.dot_general(first, b_ref[s], NT, preferred_element_type=F32)
        add_in(acc, points, slot, value)

    @pl.when(step == pl.num_programs(0) - 1)
    def _():
        u_ref[...] = acc[...].astype(BF16)


def final_body(points, counts, v_ref, e_ref, b_ref, w_ref, t_ref, o_ref):
    step = pl.program_id(0)
    for s in range(STEP):
        slot = step * STEP + s
        live = (slot < counts[0]).astype(F32)
        back = back_of(points, slot, w_ref, b_ref[s])
        second = (e_ref[s : s + 1] - 2.0) * t_ref[s].astype(F32) + (back - v_ref[s].astype(F32)) * live
        o_ref[s] = second.astype(BF16)


def fine_call(body, name, args, outs, acc):
    points, counts, *rest = args
    slots = points.shape[0]

    def spec(shape):
        if shape[0] == slots:
            zeros = (0,) * (len(shape) - 1)
            return pl.BlockSpec((STEP,) + shape[1:], lambda i, *_: (i,) + zeros)
        return pl.BlockSpec(shape, lambda i, *_: (0,) * len(shape))

    return pl.pallas_call(
        body,
        name=name,
        out_shape=outs,
        grid_spec=pltpu.PrefetchScalarGridSpec(
            num_scalar_prefetch=2,
            grid=(slots // STEP,),
            in_specs=[spec(a.shape) for a in rest],
            out_specs=jax.tree.map(lambda o: spec(o.shape), outs),
            scratch_shapes=[pltpu.VMEM((64, 2, 64, 128), F32)] if acc else [],
        ),
        compiler_params=pltpu.CompilerParams(dimension_semantics=("arbitrary",), vmem_limit_bytes=40 << 20),
    )(*args)


def local(vectors, energies, blocks, kernel, slot_coarse_kpoint, counts):
    v = vectors.transpose(0, 2, 1)
    coarse_shape = jax.ShapeDtypeStruct((64, 2, 64, 128), BF16)
    fine_shape = jax.ShapeDtypeStruct(v.shape, BF16)
    u = fine_call(project_body, "project", (slot_coarse_kpoint, counts, v, blocks), coarse_shape, True)
    w = coarse(u, kernel)
    t, u = fine_call(middle_body, "middle", (slot_coarse_kpoint, counts, v, energies, blocks, w), (fine_shape, coarse_shape), True)
    w = coarse(u, kernel)
    out = fine_call(final_body, "final", (slot_coarse_kpoint, counts, v, energies, blocks, w, t), fine_shape, False)
    return out.transpose(0, 2, 1)


def solution(mesh):
    both = ("row", "col")
    in_specs = (P(both, None, None), P(both, None), P(both, None, None), P("row", "col"), P(both), P(both))
    return jax.shard_map(local, mesh=mesh, in_specs=in_specs, out_specs=P(both, None, None), check_vma=False)
```

```python
import functools

import jax
import jax.numpy as jnp
from jax import lax
from jax.experimental import pallas as pl
from jax.experimental.pallas import tpu as pltpu
from jax.sharding import PartitionSpec as P

MESH = pl.DeviceIdType.MESH
F32 = jnp.float32
BF16 = jnp.bfloat16
STEP = 8
FINE_VMEM = 26 << 20
X, Y, Z = 0, 1, 2
GROUPS = ((slice(0, 3), X, Y, Z), (slice(3, 6), Y, Z, X), (slice(6, 8), Z, X, Y))
FAR, NEAR = (2, 1, 3, 0), (0, 1, 3, 2)
STEPS = [(i, j) for i in NEAR for j in NEAR][1:]
NT = (((1,), (1,)), ((), ()))


def position():
    r, c = lax.axis_index("row"), lax.axis_index("col")
    return (c // 2, r // 4, r % 4, c % 2)


def device(x, y, z, k):
    return (y * 4 + z, x * 2 + k)


def coarse_body(u_ref, kv, w_ref, core_in, s1, r1, s2, r2, ub, ul, prod, pw, rw,
                core_ss, core_rs, big_ss, big_rs, pl_ss, pl_rs, yz_ss, yz_rs, pr_ss, pr_rs, ap_ss, ap_rs, ab_ss, ab_rs, fin_ss, fin_rs):
    here = position()
    x, y, z, k = here

    def peer(*moves):
        there = list(here)
        for dim, step in moves:
            there[dim] = (there[dim] + step) % (4 if dim < 3 else 2)
        return device(*there)

    def send(src, dst, ss, rs, to):
        copy = pltpu.make_async_remote_copy(src_ref=src, dst_ref=dst, send_sem=ss, recv_sem=rs, device_id=to, device_id_type=MESH)
        copy.start()
        return copy

    def natural(fixed):
        return tuple(fixed.get(d, slice(None)) for d in range(3))

    xk_steps = [(i // 2, i % 2) for i in range(1, 8)]
    near = [((d, o),) for d in range(3) for o in (1, 2, 3)]
    near += [((a, i), (b, j)) for a, b in ((X, Y), (Y, Z), (Z, X)) for i in (1, 2, 3) for j in (1, 2, 3)]
    near += [((3, 1),)] + [((X, o), (3, 1)) for o in (1, 2, 3)]
    barrier = pltpu.get_barrier_semaphore()
    for moves in near:
        pl.semaphore_signal(barrier, inc=1, device_id=peer(*moves), device_id_type=MESH)
    pl.semaphore_wait(barrier, len(near))

    sent = []
    core, big, plane = {}, {}, {}
    for r in FAR:
        for g, (v, c, a, b) in enumerate(GROUPS):
            ix = natural({a: (here[a] + r) % 4})
            core[g, r] = send(u_ref.at[ix[0], 1 - k, ix[1], ix[2], v], core_in.at[ix + (v,)], core_ss.at[g, r], core_rs.at[g, r], peer((3, 1)))
            sent.append(core[g, r])
    for r in FAR:
        for g, (v, c, a, b) in enumerate(GROUPS):
            row = (here[a] + r) % 4
            ix = natural({a: row})
            core[g, r].wait_recv()
            s1[ix + (v,)] = (u_ref[ix[0], k, ix[1], ix[2], v].astype(F32) + core_in[ix + (v,)].astype(F32)).astype(BF16)
            for o in (2, 1, 3):
                src = s1.at[natural({a: row, c: (here[c] + o) % 4}) + (v,)]
                dst = r1.at[g, o - 1, row, :, pl.ds(0, v.stop - v.start)]
                big[g, r, o] = send(src, dst, big_ss.at[g, r, o - 1], big_rs.at[g, r, o - 1], peer((c, o)))
                sent.append(big[g, r, o])
    for r in FAR:
        for g, (v, c, a, b) in enumerate(GROUPS):
            n = v.stop - v.start
            row = (here[a] + r) % 4
            for o in (1, 3, 2):
                big[g, r, o].wait_recv()
            total = s1[natural({a: row, c: here[c]}) + (v,)].astype(F32)
            for o in (1, 3, 2):
                total = total + r1[g, o - 1, row, :, :n].astype(F32)
            s2[g, row, :, :n] = total.astype(BF16)
            for j in FAR:
                if (r, j) != (0, 0):
                    i = STEPS.index((r, j))
                    plane[g, r, j] = send(s2.at[g, row, (here[b] + j) % 4, pl.ds(0, n)], r2.at[g, i, pl.ds(0, n)], pl_ss.at[g, i], pl_rs.at[g, i], peer((a, r), (b, j)))
                    sent.append(plane[g, r, j])
    for g, (v, c, a, b) in enumerate(GROUPS):
        n = v.stop - v.start
        total = s2[g, here[a], here[b], :n].astype(F32)
        for i, step in enumerate(STEPS):
            plane[(g,) + step].wait_recv()
            total = total + r2[g, i, :n].astype(F32)
        ub[y, z, v] = total.astype(BF16)
    spread = {}
    for i, (p, q) in enumerate(STEPS):
        spread[p, q] = send(ub.at[y, z], ub.at[y, z], yz_ss.at[i], yz_rs.at[i], peer((Y, p), (Z, q)))
        sent.append(spread[p, q])
    for first, r in enumerate(NEAR):
        row = (y + r) % 4
        for q in range(4):
            if (r, q) != (0, 0):
                spread[(-r) % 4, (-q) % 4].wait_recv()
        for q in range(4):
            ul[:, q * 128 : q * 128 + 128] = ub[row, q].reshape(64, 128)
        for n in range(4):
            rows = slice(n * 256, n * 256 + 256)
            part = lax.dot_general(ul[...], kv[rows, pl.ds(pl.multiple_of(row * 512, 512), 512)], NT, preferred_element_type=F32)
            prod[:, rows] = part if first == 0 else prod[:, rows] + part
    for n in range(8):
        pw[n // 2, n % 2] = prod[:, n * 128 : n * 128 + 128].astype(BF16).reshape(8, 8, 128)
    swap = [send(pw.at[(x + p) % 4, (k + q) % 2], rw.at[i], pr_ss.at[i], pr_rs.at[i], peer((X, p), (3, q))) for i, (p, q) in enumerate(xk_steps)]
    sent += swap
    total = pw[x, k].astype(F32)
    for i in range(7):
        swap[i].wait_recv()
        total = total + rw[i].astype(F32)
    w_ref[y, z, x, k] = total.astype(BF16)

    def part_of(v, fixed):
        ix = natural(fixed)
        return w_ref.at[ix[1], ix[2], ix[0], k, v]

    plane, big, last = {}, {}, []
    for i, (p, q) in enumerate(STEPS):
        for g, (v, c, a, b) in enumerate(GROUPS):
            block = part_of(v, {d: here[d] for d in range(3)})
            plane[g, p, q] = send(block, block, ap_ss.at[g, i], ap_rs.at[g, i], peer((a, p), (b, q)))
            sent.append(plane[g, p, q])
    for r in NEAR:
        for g, (v, c, a, b) in enumerate(GROUPS):
            for q in range(4):
                if (r, q) != (0, 0):
                    plane[g, (-r) % 4, (-q) % 4].wait_recv()
            block = part_of(v, {a: (here[a] + r) % 4, c: here[c]})
            for o in (2, 1, 3):
                big[g, r, o] = send(block, block, ab_ss.at[g, r, o - 1], ab_rs.at[g, r, o - 1], peer((c, o)))
                sent.append(big[g, r, o])
    for r in NEAR:
        for g, (v, c, a, b) in enumerate(GROUPS):
            for o in (1, 3, 2):
                big[g, r, o].wait_recv()
            block = part_of(v, {a: (here[a] + r) % 4})
            last.append(send(block, block, fin_ss.at[g, r], fin_rs.at[g, r], peer((3, 1))))
    for copy in last:
        copy.wait_recv()
    for copy in sent + last:
        copy.wait_send()


def coarse(part, kernel):
    dma = pltpu.SemaphoreType.DMA
    tile = (8, 128)
    whole = pl.pallas_call(
        coarse_body,
        name="coarse",
        out_shape=jax.ShapeDtypeStruct((4, 4, 4, 2, 8) + tile, BF16),
        in_specs=[pl.BlockSpec(memory_space=pltpu.VMEM)] * 2,
        out_specs=pl.BlockSpec(memory_space=pltpu.VMEM),
        scratch_shapes=[
            pltpu.VMEM((4, 4, 4, 8) + tile, BF16),
            pltpu.VMEM((4, 4, 4, 8) + tile, BF16),
            pltpu.VMEM((3, 3, 4, 4, 3) + tile, BF16),
            pltpu.VMEM((3, 4, 4, 3) + tile, BF16),
            pltpu.VMEM((3, 15, 3) + tile, BF16),
            pltpu.VMEM((4, 4, 8) + tile, BF16),
            pltpu.VMEM((64, 512), BF16),
            pltpu.VMEM((64, 1024), F32),
            pltpu.VMEM((4, 2, 8) + tile, BF16),
            pltpu.VMEM((7, 8) + tile, BF16),
        ]
        + [dma(s) for s in ((3, 4), (3, 4, 3), (3, 15), (15,), (7,), (3, 15), (3, 4, 3), (3, 4)) for _ in range(2)],
        compiler_params=pltpu.CompilerParams(collective_id=0, has_side_effects=True, vmem_limit_bytes=10 << 20),
    )(part.reshape((4, 2, 4, 4, 8) + tile), kernel)
    return whole.reshape(64, 2, 64, 128)


def add_in(acc, points, slot, value):
    p = points[slot]
    acc[p, 0] += value[:, :128]
    acc[p, 1] += value[:, 128:]


def back_of(points, slot, w_ref, b):
    p = points[slot]
    w = jnp.concatenate([w_ref[p, 0], w_ref[p, 1]], axis=1)
    return jnp.dot(w, b, preferred_element_type=F32)


def project_body(points, counts, v_hbm, b_hbm, u_ref, b_ref, acc, v_ref, v_sem, b_sem):
    def chunk(i):
        rows = pl.ds(i * STEP, STEP)
        return (
            pltpu.make_async_copy(v_hbm.at[rows], v_ref.at[rows], v_sem.at[i]),
            pltpu.make_async_copy(b_hbm.at[rows], b_ref.at[rows], b_sem.at[i]),
        )

    chunks = b_ref.shape[0] // STEP
    for i in range(chunks):
        for copy in chunk(i):
            copy.start()
    acc[...] = jnp.zeros_like(acc)

    @pl.loop(0, chunks)
    def _(i):
        for copy in chunk(i):
            copy.wait()
        for s in range(STEP):
            slot = i * STEP + s
            live = (slot < counts[0]).astype(BF16)
            value = lax.dot_general(v_ref[slot] * live, b_ref[slot], NT, preferred_element_type=F32)
            add_in(acc, points, slot, value)

    u_ref[...] = acc[...].astype(BF16)


def middle_body(points, counts, v_ref, e_ref, b_ref, w_ref, t_ref, u_ref, acc):
    acc[...] = jnp.zeros_like(acc)

    @pl.loop(0, b_ref.shape[0] // STEP)
    def _(i):
        gain = e_ref[pl.ds(pl.multiple_of(i * STEP, STEP), STEP)] - 2.0
        for s in range(STEP):
            slot = i * STEP + s
            live = (slot < counts[0]).astype(F32)
            back = back_of(points, slot, w_ref, b_ref[slot])
            start = v_ref[slot].astype(F32)
            first = ((gain[s : s + 1] * start + back) * (0.5 * live)).astype(BF16)
            t_ref[slot] = first
            value = lax.dot_general(first, b_ref[slot], NT, preferred_element_type=F32)
            add_in(acc, points, slot, value)

    u_ref[...] = acc[...].astype(BF16)


def final_body(points, counts, v_ref, e_ref, b_ref, w_ref, t_ref, o_hbm, o_ref, o_sem):
    def chunk(i):
        rows = pl.ds(i * STEP, STEP)
        return pltpu.make_async_copy(o_ref.at[rows], o_hbm.at[rows], o_sem.at[i])

    chunks = b_ref.shape[0] // STEP

    @pl.loop(0, chunks)
    def _(i):
        gain = e_ref[pl.ds(pl.multiple_of(i * STEP, STEP), STEP)] - 2.0
        for s in range(STEP):
            slot = i * STEP + s
            live = (slot < counts[0]).astype(F32)
            back = back_of(points, slot, w_ref, b_ref[slot])
            second = gain[s : s + 1] * t_ref[slot].astype(F32) + (back - v_ref[slot].astype(F32)) * live
            o_ref[slot] = second.astype(BF16)
        chunk(i).start()

    for i in range(chunks):
        chunk(i).wait()


def fine_call(body, name, args, outs, ins, out_specs, scratch):
    smem = pl.BlockSpec(memory_space=pltpu.SMEM)
    return pl.pallas_call(
        body,
        name=name,
        out_shape=outs,
        in_specs=[smem, smem] + ins,
        out_specs=out_specs,
        scratch_shapes=scratch,
        compiler_params=pltpu.CompilerParams(vmem_limit_bytes=FINE_VMEM),
    )(*args)


def local(vectors, energies, blocks, kernel, slot_coarse_kpoint, counts):
    v = vectors.transpose(0, 2, 1)
    chunks = v.shape[0] // STEP
    table = (slot_coarse_kpoint, counts)
    coarse_shape = jax.ShapeDtypeStruct((64, 2, 64, 128), BF16)
    fine_shape = jax.ShapeDtypeStruct(v.shape, BF16)
    block_shape = jax.ShapeDtypeStruct(blocks.shape, BF16)
    acc = pltpu.VMEM(coarse_shape.shape, F32)
    vmem = pl.BlockSpec(memory_space=pltpu.VMEM)
    dma = pltpu.SemaphoreType.DMA
    u, held = fine_call(project_body, "project", table + (v, blocks), (coarse_shape, block_shape), [pl.BlockSpec(memory_space=pltpu.HBM)] * 2, (vmem, vmem),
                        [acc, pltpu.VMEM(v.shape, BF16), dma((chunks,)), dma((chunks,))])
    w = coarse(u, kernel)
    t, u = fine_call(middle_body, "middle", table + (v, energies, held, w), (fine_shape, coarse_shape), [vmem] * 4, (vmem, vmem), [acc])
    w = coarse(u, kernel)
    out = fine_call(final_body, "final", table + (v, energies, held, w, t), fine_shape, [vmem] * 5, pl.BlockSpec(memory_space=pltpu.HBM),
                    [pltpu.VMEM(v.shape, BF16), dma((chunks,))])
    return out.transpose(0, 2, 1)


def solution(mesh):
    both = ("row", "col")
    in_specs = (P(both, None, None), P(both, None), P(both, None, None), P("row", "col"), P(both), P(both))
    return jax.shard_map(local, mesh=mesh, in_specs=in_specs, out_specs=P(both, None, None), check_vma=False)
```

```python
import functools

import jax
import jax.numpy as jnp
from jax import lax
from jax.experimental import pallas as pl
from jax.experimental.pallas import tpu as pltpu
from jax.sharding import PartitionSpec as P

MESH = pl.DeviceIdType.MESH
F32 = jnp.float32
BF16 = jnp.bfloat16
STEP = 8
MAIN_VMEM = 22 << 20
FINAL_VMEM = 8 << 20
X, Y, Z = 0, 1, 2
GROUPS = ((slice(0, 3), X, Y, Z), (slice(3, 6), Y, Z, X), (slice(6, 8), Z, X, Y))
FAR, NEAR = (2, 1, 3, 0), (0, 1, 3, 2)
STEPS = [(i, j) for i in NEAR for j in NEAR][1:]
NT = (((1,), (1,)), ((), ()))


def position():
    r, c = lax.axis_index("row"), lax.axis_index("col")
    return (lax.div(c, 2), lax.div(r, 4), lax.rem(r, 4), lax.rem(c, 2))


def moved(here, moves):
    there = list(here)
    for dim, step in moves:
        there[dim] = 1 - there[dim] if dim == 3 else lax.rem(there[dim] + step, 4)
    return there


def device(here, moves):
    x, y, z, k = moved(here, moves)
    return (y * 4 + z, x * 2 + k)


def natural(fixed):
    return tuple(fixed.get(d, slice(None)) for d in range(3))


SIBLING = (3, 1)
XK = [((X, i),) if not q else ((X, i), SIBLING) if i else (SIBLING,) for i in range(4) for q in range(2)][1:]
PEERS = [((d, o),) for d in range(3) for o in (1, 2, 3)]
PEERS += [((a, i), (b, j)) for a, b in ((X, Y), (Y, Z), (Z, X)) for i in (1, 2, 3) for j in (1, 2, 3)]
PEERS += [(SIBLING,)] + [((X, o), SIBLING) for o in (1, 2, 3)]


def greet(here):
    barrier = pltpu.get_barrier_semaphore()
    for moves in PEERS:
        pl.semaphore_signal(barrier, inc=1, device_id=device(here, moves), device_id_type=MESH)


def greeted():
    pl.semaphore_wait(pltpu.get_barrier_semaphore(), len(PEERS))


def send(here, src, dst, ss, rs, moves):
    pltpu.make_async_remote_copy(src_ref=src, dst_ref=dst, send_sem=ss, recv_sem=rs, device_id=device(here, moves), device_id_type=MESH).start()


def landed(here, ref, rs):
    pltpu.make_async_remote_copy(src_ref=ref, dst_ref=ref, send_sem=rs, recv_sem=rs, device_id=device(here, (SIBLING,)), device_id_type=MESH).wait_recv()


def gone(here, ref, ss):
    pltpu.make_async_remote_copy(src_ref=ref, dst_ref=ref, send_sem=ss, recv_sem=ss, device_id=device(here, (SIBLING,)), device_id_type=MESH).wait_send()


def moves_of(*pairs):
    return tuple(p for p in pairs if p[1])


def coarse_round(here, u_ref, kv, w_ref, core_in, s1, r1, s2, r2, ub, ul, prod, pw, rw, sems):
    (core_ss, core_rs, big_ss, big_rs, pl_ss, pl_rs, yz_ss, yz_rs, pr_ss, pr_rs, ap_ss, ap_rs, ab_ss, ab_rs, fin_ss, fin_rs) = sems
    x, y, z, k = here
    along = [[moved(here, ((d, o),))[d] for o in range(4)] for d in range(3)]

    for r in FAR:
        for g, (v, c, a, b) in enumerate(GROUPS):
            ix = natural({a: along[a][r]})
            send(here, u_ref.at[ix[0], 1 - k, ix[1], ix[2], v], core_in.at[ix + (v,)], core_ss, core_rs.at[g, r], (SIBLING,))
    for r in FAR:
        for g, (v, c, a, b) in enumerate(GROUPS):
            ix = natural({a: along[a][r]})
            landed(here, core_in.at[ix + (v,)], core_rs.at[g, r])
            s1[ix + (v,)] = (u_ref[ix[0], k, ix[1], ix[2], v].astype(F32) + core_in[ix + (v,)].astype(F32)).astype(BF16)
            for o in (2, 1, 3):
                src = s1.at[natural({a: along[a][r], c: along[c][o]}) + (v,)]
                send(here, src, r1.at[o - 1, along[a][r], :, v], big_ss, big_rs.at[g, r], ((c, o),))
    for r in FAR:
        for g, (v, c, a, b) in enumerate(GROUPS):
            row = along[a][r]
            landed(here, r1.at[:, row, :, v], big_rs.at[g, r])
            total = s1[natural({a: row, c: here[c]}) + (v,)].astype(F32)
            for o in range(3):
                total = total + r1[o, row, :, v].astype(F32)
            s2[row, :, v] = total.astype(BF16)
            for j in FAR:
                if (r, j) != (0, 0):
                    send(here, s2.at[row, along[b][j], v], r2.at[STEPS.index((r, j)), v], pl_ss, pl_rs.at[g], moves_of((a, r), (b, j)))
    for g, (v, c, a, b) in enumerate(GROUPS):
        landed(here, r2.at[:, v], pl_rs.at[g])
        total = s2[here[a], here[b], v].astype(F32)
        for i in range(15):
            total = total + r2[i, v].astype(F32)
        ub[y, z, v] = total.astype(BF16)
    for p, q in STEPS:
        send(here, ub.at[y, z], ub.at[y, z], yz_ss, yz_rs.at[p], moves_of((Y, p), (Z, q)))
    for first, r in enumerate(NEAR):
        row = along[Y][r]
        landed(here, ub.at[row] if r else ub.at[row, pl.ds(0, 3)], yz_rs.at[(-r) % 4])
        for q in range(4):
            ul[:, q * 128 : q * 128 + 128] = ub[row, q].reshape(64, 128)
        for n in range(4):
            rows = slice(n * 256, n * 256 + 256)
            part = lax.dot_general(ul[...], kv[rows, pl.ds(pl.multiple_of(row * 512, 512), 512)], NT, preferred_element_type=F32)
            prod[:, rows] = part if first == 0 else prod[:, rows] + part
    for n in range(8):
        pw[n // 2, n % 2] = prod[:, n * 128 : n * 128 + 128].astype(BF16).reshape(8, 8, 128)
    for i, moves in enumerate(XK):
        there = moved(here, moves)
        send(here, pw.at[there[0], there[3]], rw.at[i], pr_ss, pr_rs, moves)
    landed(here, rw, pr_rs)
    total = pw[x, k].astype(F32)
    for i in range(7):
        total = total + rw[i].astype(F32)
    w_ref[y, z, x, k] = total.astype(BF16)

    def part_of(v, fixed):
        ix = natural(fixed)
        return w_ref.at[ix[1], ix[2], ix[0], k, v]

    for p, q in STEPS:
        for g, (v, c, a, b) in enumerate(GROUPS):
            block = part_of(v, {d: here[d] for d in range(3)})
            send(here, block, block, ap_ss, ap_rs.at[g, p], moves_of((a, p), (b, q)))
    some = pl.ds(0, 3)
    for r in NEAR:
        for g, (v, c, a, b) in enumerate(GROUPS):
            row = {a: along[a][r], c: here[c]}
            landed(here, part_of(v, row if r else row | {b: some}), ap_rs.at[g, (-r) % 4])
            block = part_of(v, row)
            for o in (2, 1, 3):
                send(here, block, block, ab_ss, ab_rs.at[g, r], ((c, o),))
    for r in NEAR:
        for g, (v, c, a, b) in enumerate(GROUPS):
            row = {a: along[a][r]}
            landed(here, part_of(v, row | {c: some}), ab_rs.at[g, r])
            block = part_of(v, row)
            send(here, block, block, fin_ss, fin_rs, (SIBLING,))
    landed(here, w_ref.at[:, :, :, 1 - k], fin_rs)
    gone(here, core_in, core_ss)
    gone(here, s1.at[some], big_ss)
    gone(here, r2, pl_ss)
    gone(here, r2, yz_ss)
    gone(here, rw, pr_ss)
    gone(here, r2, ap_ss)
    gone(here, w_ref.at[some, :, :, 0], ab_ss)
    gone(here, w_ref.at[:, :, :, 0], fin_ss)


ROUND = [
    pltpu.VMEM((4, 4, 4, 8, 8, 128), BF16),
    pltpu.VMEM((4, 4, 4, 8, 8, 128), BF16),
    pltpu.VMEM((3, 4, 4, 8, 8, 128), BF16),
    pltpu.VMEM((4, 4, 8, 8, 128), BF16),
    pltpu.VMEM((15, 8, 8, 128), BF16),
    pltpu.VMEM((4, 4, 8, 8, 128), BF16),
    pltpu.VMEM((64, 512), BF16),
    pltpu.VMEM((64, 1024), F32),
    pltpu.VMEM((4, 2, 8, 8, 128), BF16),
    pltpu.VMEM((7, 8, 8, 128), BF16),
]
SEMS = [pltpu.SemaphoreType.DMA(s) for n in ((3, 4), (3, 4), (3,), (4,), (), (3, 4), (3, 4), ()) for s in ((), n)]


def back_of(points, slot, w_ref, b):
    p = points[slot]
    w = jnp.concatenate([w_ref[p, 0], w_ref[p, 1]], axis=1)
    return jnp.dot(w, b, preferred_element_type=F32)


def main_body(points, counts, links, v_hbm, e_hbm, b_hbm, k_hbm, t_ref, b_ref, w_ref,
              v_ref, e_ref, kv, sums, u_ref, v_sem, b_sem, e_sem, k_sem, *scratch):
    here = position()
    slots = b_ref.shape[0]
    chunks = slots // STEP
    greet(here)

    def chunk(i):
        rows = pl.ds(i * STEP, STEP)
        return (
            pltpu.make_async_copy(v_hbm.at[rows], v_ref.at[rows], v_sem.at[i]),
            pltpu.make_async_copy(b_hbm.at[rows], b_ref.at[rows], b_sem.at[i]),
        )

    for i in range(chunks):
        for copy in chunk(i):
            copy.start()
    energies = pltpu.make_async_copy(e_hbm, e_ref, e_sem)
    energies.start()
    table = pltpu.make_async_copy(k_hbm, kv, k_sem)
    table.start()
    sums[0] = jnp.zeros(sums.shape[1:], F32)

    def gather():
        @pl.loop(0, 64, unroll=2)
        def _(p):
            value = sums[links[slots + p]].astype(BF16)
            u_ref[p, 0] = value[:, :128].reshape(8, 8, 128)
            u_ref[p, 1] = value[:, 128:].reshape(8, 8, 128)

    @pl.loop(0, chunks)
    def _(i):
        for copy in chunk(i):
            copy.wait()
        for s in range(STEP):
            slot = i * STEP + s
            live = (slot < counts[0]).astype(BF16)
            value = lax.dot_general(v_ref[slot] * live, b_ref[slot], NT, preferred_element_type=F32)
            sums[slot + 1] = value + sums[links[slot]]

    gather()
    energies.wait()
    table.wait()
    greeted()
    u_view = u_ref.reshape(4, 2, 4, 4, 8, 8, 128)
    round_of = lambda: coarse_round(here, u_view, kv, w_ref, *scratch[: len(ROUND)], scratch[len(ROUND) :])
    round_of()
    w_view = w_ref.reshape(64, 2, 64, 128)

    @pl.loop(0, chunks)
    def _(i):
        gain = e_ref[pl.ds(pl.multiple_of(i * STEP, STEP), STEP)] - 2.0
        for s in range(STEP):
            slot = i * STEP + s
            live = (slot < counts[0]).astype(F32)
            back = back_of(points, slot, w_view, b_ref[slot])
            start = v_ref[slot].astype(F32)
            first = ((gain[s : s + 1] * start + back) * (0.5 * live)).astype(BF16)
            t_ref[slot] = first
            value = lax.dot_general(first, b_ref[slot], NT, preferred_element_type=F32)
            sums[slot + 1] = value + sums[links[slot]]

    gather()
    round_of()


def final_body(points, counts, v_ref, e_ref, b_ref, w_ref, t_ref, o_hbm, o_ref, o_sem):
    def chunk(i):
        rows = pl.ds(i * STEP, STEP)
        return pltpu.make_async_copy(o_ref.at[rows], o_hbm.at[rows], o_sem.at[i])

    chunks = b_ref.shape[0] // STEP

    @pl.loop(0, chunks)
    def _(i):
        gain = e_ref[pl.ds(pl.multiple_of(i * STEP, STEP), STEP)] - 2.0
        for s in range(STEP):
            slot = i * STEP + s
            live = (slot < counts[0]).astype(F32)
            back = back_of(points, slot, w_ref, b_ref[slot])
            second = gain[s : s + 1] * t_ref[slot].astype(F32) + (back - v_ref[slot].astype(F32)) * live
            o_ref[slot] = second.astype(BF16)
        chunk(i).start()

    for i in range(chunks):
        chunk(i).wait()


def local(vectors, energies, blocks, kernel, slot_coarse_kpoint, counts):
    v = vectors.transpose(0, 2, 1)
    slots = v.shape[0]
    chunks = slots // STEP
    query = lax.broadcasted_iota(jnp.int32, (slots + 64, slots), 0)
    order = lax.broadcasted_iota(jnp.int32, (slots + 64, slots), 1)
    point = jnp.pad(slot_coarse_kpoint, (0, 64))[:, None] + jnp.maximum(query - slots, 0)
    match = (point == slot_coarse_kpoint[None, :]) & (order < query)
    links = jnp.max(jnp.where(match, order + 1, 0), axis=1)
    coarse_shape = jax.ShapeDtypeStruct((4, 4, 4, 2, 8, 8, 128), BF16)
    fine_shape = jax.ShapeDtypeStruct(v.shape, BF16)
    block_shape = jax.ShapeDtypeStruct(blocks.shape, BF16)
    smem, vmem, hbm = (pl.BlockSpec(memory_space=m) for m in (pltpu.SMEM, pltpu.VMEM, pltpu.HBM))
    dma = pltpu.SemaphoreType.DMA
    t, held, w = pl.pallas_call(
        main_body,
        name="main",
        out_shape=(fine_shape, block_shape, coarse_shape),
        in_specs=[smem] * 3 + [hbm] * 4,
        out_specs=(vmem, vmem, vmem),
        scratch_shapes=[
            pltpu.VMEM(v.shape, BF16),
            pltpu.VMEM(energies.shape, F32),
            pltpu.VMEM(kernel.shape, BF16),
            pltpu.VMEM((slots + 1, 64, 256), F32),
            pltpu.VMEM((64, 2, 8, 8, 128), BF16),
            dma((chunks,)), dma((chunks,)), dma, dma,
        ] + ROUND + SEMS,
        compiler_params=pltpu.CompilerParams(collective_id=0, has_side_effects=True, vmem_limit_bytes=MAIN_VMEM),
    )(slot_coarse_kpoint, counts, links, *(pltpu.with_memory_space_constraint(a, pltpu.HBM) for a in (v, energies, blocks, kernel)))
    out = pl.pallas_call(
        final_body,
        name="final",
        out_shape=fine_shape,
        in_specs=[smem] * 2 + [vmem] * 5,
        out_specs=hbm,
        scratch_shapes=[pltpu.VMEM(v.shape, BF16), dma((chunks,))],
        compiler_params=pltpu.CompilerParams(vmem_limit_bytes=FINAL_VMEM),
    )(slot_coarse_kpoint, counts, v, energies, held, w.reshape(64, 2, 64, 128), t)
    return out.transpose(0, 2, 1)


def solution(mesh):
    both = ("row", "col")
    in_specs = (P(both, None, None), P(both, None), P(both, None, None), P("row", "col"), P(both), P(both))
    return jax.shard_map(local, mesh=mesh, in_specs=in_specs, out_specs=P(both, None, None), check_vma=False)
```

```python
import functools

import jax
import jax.numpy as jnp
from jax import lax
from jax.experimental import pallas as pl
from jax.experimental.pallas import tpu as pltpu
from jax.sharding import PartitionSpec as P

MESH = pl.DeviceIdType.MESH
F32 = jnp.float32
BF16 = jnp.bfloat16
STEP, MIDDLE, FINAL = 16, 24, 32
MAIN_VMEM = 22 << 20
FINAL_VMEM = 8 << 20
X, Y, Z = 0, 1, 2
GROUPS = ((slice(0, 3), X, Y, Z), (slice(3, 6), Y, Z, X), (slice(6, 8), Z, X, Y))
FAR, NEAR = (2, 1, 3, 0), (0, 1, 3, 2)
STEPS = [(i, j) for i in NEAR for j in NEAR][1:]
NT = (((1,), (1,)), ((), ()))


def position():
    r, c = lax.axis_index("row"), lax.axis_index("col")
    return (lax.div(c, 2), lax.div(r, 4), lax.rem(r, 4), lax.rem(c, 2))


def moved(here, moves):
    there = list(here)
    for dim, step in moves:
        there[dim] = 1 - there[dim] if dim == 3 else lax.rem(there[dim] + step, 4)
    return there


def device(here, moves):
    x, y, z, k = moved(here, moves)
    return (y * 4 + z, x * 2 + k)


def natural(fixed):
    return tuple(fixed.get(d, slice(None)) for d in range(3))


SIBLING = (3, 1)
XK = [((X, i),) * (i > 0) + (SIBLING,) * q for i in range(4) for q in range(2)][1:]
PEERS = [((d, o),) for d in range(3) for o in (1, 2, 3)]
PEERS += [((a, i), (b, j)) for a, b in ((X, Y), (Y, Z), (Z, X)) for i in (1, 2, 3) for j in (1, 2, 3)]
PEERS += [(SIBLING,)] + [((X, o), SIBLING) for o in (1, 2, 3)]


def greet(here):
    barrier = pltpu.get_barrier_semaphore()
    for moves in PEERS:
        pl.semaphore_signal(barrier, inc=1, device_id=device(here, moves), device_id_type=MESH)


def greeted():
    pl.semaphore_wait(pltpu.get_barrier_semaphore(), len(PEERS))


def send(here, src, dst, ss, rs, moves):
    pltpu.make_async_remote_copy(src_ref=src, dst_ref=dst, send_sem=ss, recv_sem=rs, device_id=device(here, moves), device_id_type=MESH).start()


def landed(here, ref, rs):
    pltpu.make_async_remote_copy(src_ref=ref, dst_ref=ref, send_sem=rs, recv_sem=rs, device_id=device(here, (SIBLING,)), device_id_type=MESH).wait_recv()


def gone(here, ref, ss):
    pltpu.make_async_remote_copy(src_ref=ref, dst_ref=ref, send_sem=ss, recv_sem=ss, device_id=device(here, (SIBLING,)), device_id_type=MESH).wait_send()


def moves_of(*pairs):
    return tuple(p for p in pairs if p[1])


def coarse_round(here, u_ref, own_half, kv, w_ref, core_in, s1, r1, s2, r2, ub, ul, prod, pw, rw, sems):
    (core_ss, core_rs, big_ss, big_rs, pl_ss, pl_rs, yz_ss, yz_rs, pr_ss, pr_rs, ap_ss, ap_rs, ab_ss, ab_rs, fin_ss, fin_rs) = sems
    x, y, z, k = here
    along = [[moved(here, ((d, o),))[d] for o in range(4)] for d in range(3)]

    for r in FAR:
        for g, (v, c, a, b) in enumerate(GROUPS):
            ix = natural({a: along[a][r]})
            send(here, u_ref.at[ix[0], 1 - k, ix[1], ix[2], v], core_in.at[ix + (v,)], core_ss, core_rs.at[g, r], (SIBLING,))
    own_half()
    for r in FAR:
        for g, (v, c, a, b) in enumerate(GROUPS):
            ix = natural({a: along[a][r]})
            landed(here, core_in.at[ix + (v,)], core_rs.at[g, r])
            s1[ix + (v,)] = (u_ref[ix[0], k, ix[1], ix[2], v].astype(F32) + core_in[ix + (v,)].astype(F32)).astype(BF16)
            for o in (2, 1, 3):
                src = s1.at[natural({a: along[a][r], c: along[c][o]}) + (v,)]
                send(here, src, r1.at[o - 1, along[a][r], :, v], big_ss, big_rs.at[g, r], ((c, o),))
    for r in FAR:
        for g, (v, c, a, b) in enumerate(GROUPS):
            row = along[a][r]
            landed(here, r1.at[:, row, :, v], big_rs.at[g, r])
            total = s1[natural({a: row, c: here[c]}) + (v,)].astype(F32)
            for o in range(3):
                total = total + r1[o, row, :, v].astype(F32)
            s2[row, :, v] = total.astype(BF16)
            for j in FAR:
                if (r, j) != (0, 0):
                    send(here, s2.at[row, along[b][j], v], r2.at[STEPS.index((r, j)), v], pl_ss, pl_rs.at[g], moves_of((a, r), (b, j)))
    for g, (v, c, a, b) in enumerate(GROUPS):
        landed(here, r2.at[:, v], pl_rs.at[g])
        total = s2[here[a], here[b], v].astype(F32)
        for i in range(15):
            total = total + r2[i, v].astype(F32)
        ub[y, z, v] = total.astype(BF16)
    for p, q in STEPS:
        send(here, ub.at[y, z], ub.at[y, z], yz_ss, yz_rs.at[p], moves_of((Y, p), (Z, q)))
    for first, r in enumerate(NEAR):
        row = along[Y][r]
        landed(here, ub.at[row] if r else ub.at[row, pl.ds(0, 3)], yz_rs.at[(-r) % 4])
        for q in range(4):
            ul[:, q * 128 : q * 128 + 128] = ub[row, q].reshape(64, 128)
        for o in FAR:
            n = along[X][o]
            rows = pl.ds(pl.multiple_of(n * 256, 256), 256)
            part = lax.dot_general(ul[...], kv[rows, pl.ds(pl.multiple_of(row * 512, 512), 512)], NT, preferred_element_type=F32)
            part = part if first == 0 else prod[o] + part
            if first < 3:
                prod[o] = part
                continue
            for h in range(2):
                pw[n, h] = part[:, h * 128 : h * 128 + 128].astype(BF16).reshape(8, 8, 128)
            for i, moves in enumerate(XK):
                if dict(moves).get(X, 0) == o:
                    there = moved(here, moves)
                    send(here, pw.at[there[0], there[3]], rw.at[i], pr_ss, pr_rs, moves)
    landed(here, rw, pr_rs)
    total = pw[x, k].astype(F32)
    for i in range(7):
        total = total + rw[i].astype(F32)
    w_ref[y, z, x, k] = total.astype(BF16)

    def part_of(v, fixed):
        ix = natural(fixed)
        return w_ref.at[ix[1], ix[2], ix[0], k, v]

    for p, q in STEPS:
        for g, (v, c, a, b) in enumerate(GROUPS):
            block = part_of(v, {d: here[d] for d in range(3)})
            send(here, block, block, ap_ss, ap_rs.at[g, p], moves_of((a, p), (b, q)))
    some = pl.ds(0, 3)
    for r in NEAR:
        for g, (v, c, a, b) in enumerate(GROUPS):
            row = {a: along[a][r], c: here[c]}
            landed(here, part_of(v, row if r else row | {b: some}), ap_rs.at[g, (-r) % 4])
            block = part_of(v, row)
            for o in (2, 1, 3):
                send(here, block, block, ab_ss, ab_rs.at[g, r], ((c, o),))
    for r in NEAR:
        for g, (v, c, a, b) in enumerate(GROUPS):
            row = {a: along[a][r]}
            landed(here, part_of(v, row | {c: some}), ab_rs.at[g, r])
            block = part_of(v, row)
            send(here, block, block, fin_ss, fin_rs, (SIBLING,))
    landed(here, w_ref.at[:, :, :, 1 - k], fin_rs)


def coarse_sent(here, w_ref, core_in, s1, r1, s2, r2, ub, ul, prod, pw, rw, sems):
    core_ss, big_ss, pl_ss, yz_ss, pr_ss, ap_ss, ab_ss, fin_ss = sems[::2]
    some = pl.ds(0, 3)
    gone(here, core_in, core_ss)
    gone(here, s1.at[some], big_ss)
    gone(here, r2, pl_ss)
    gone(here, r2, yz_ss)
    gone(here, rw, pr_ss)
    gone(here, r2, ap_ss)
    gone(here, w_ref.at[some, :, :, 0], ab_ss)
    gone(here, w_ref.at[:, :, :, 0], fin_ss)


ROUND = [
    pltpu.VMEM((4, 4, 4, 8, 8, 128), BF16),
    pltpu.VMEM((4, 4, 4, 8, 8, 128), BF16),
    pltpu.VMEM((3, 4, 4, 8, 8, 128), BF16),
    pltpu.VMEM((4, 4, 8, 8, 128), BF16),
    pltpu.VMEM((15, 8, 8, 128), BF16),
    pltpu.VMEM((4, 4, 8, 8, 128), BF16),
    pltpu.VMEM((64, 512), BF16),
    pltpu.VMEM((4, 64, 256), F32),
    pltpu.VMEM((4, 2, 8, 8, 128), BF16),
    pltpu.VMEM((7, 8, 8, 128), BF16),
]
SEMS = [pltpu.SemaphoreType.DMA(s) for n in ((3, 4), (3, 4), (3,), (4,), (), (3, 4), (3, 4), ()) for s in ((), n)]


def back_of(points, slot, w_ref, b):
    p = points[slot]
    w = jnp.concatenate([w_ref[p, 0], w_ref[p, 1]], axis=1)
    return jnp.dot(w, b, preferred_element_type=F32)


def main_body(links, v_hbm, e_hbm, b_hbm, k_hbm, t_ref, b_ref, w_ref,
              v_ref, e_ref, kv, sums, u_ref, v_sem, b_sem, e_sem, k_sem, *scratch):
    here = position()
    slots = b_ref.shape[0]
    chunks = slots // STEP
    greet(here)

    def chunk(i):
        rows = pl.ds(i * STEP, STEP)
        return (
            pltpu.make_async_copy(v_hbm.at[rows], v_ref.at[rows], v_sem.at[i]),
            pltpu.make_async_copy(b_hbm.at[rows], b_ref.at[rows], b_sem.at[i]),
        )

    for i in range(chunks):
        for copy in chunk(i):
            copy.start()
    energies = pltpu.make_async_copy(e_hbm, e_ref, e_sem)
    energies.start()
    table = pltpu.make_async_copy(k_hbm, kv, k_sem)
    table.start()
    sums[0] = jnp.zeros(sums.shape[1:], F32)

    points, count = slots + 64, 2 * slots + 64

    def gather(half):
        @pl.loop(0, 32, unroll=2)
        def _(i):
            p = lax.div(i, 8) * 16 + half * 8 + lax.rem(i, 8)
            value = sums[links[slots + p]].astype(BF16)
            u_ref[p, 0] = value[:, :128].reshape(8, 8, 128)
            u_ref[p, 1] = value[:, 128:].reshape(8, 8, 128)

    @pl.loop(0, chunks)
    def _(i):
        for copy in chunk(i):
            copy.wait()
        for s in range(STEP):
            slot = i * STEP + s
            live = (slot < links[count]).astype(BF16)
            value = lax.dot_general(v_ref[slot] * live, b_ref[slot], NT, preferred_element_type=F32)
            sums[slot + 1] = value + sums[links[slot]]

    gather(1 - here[3])
    energies.wait()
    table.wait()
    greeted()
    u_view = u_ref.reshape(4, 2, 4, 4, 8, 8, 128)
    buffers, sems = scratch[: len(ROUND)], scratch[len(ROUND) :]
    coarse_round(here, u_view, lambda: gather(here[3]), kv, w_ref, *buffers, sems)
    w_view = w_ref.reshape(64, 2, 64, 128)

    @pl.loop(0, slots // MIDDLE)
    def _(i):
        gain = e_ref[pl.ds(pl.multiple_of(i * MIDDLE, 8), MIDDLE)] - 2.0
        for s in range(MIDDLE):
            slot = i * MIDDLE + s
            live = (slot < links[count]).astype(F32)
            back = back_of(links, points + slot, w_view, b_ref[slot])
            start = v_ref[slot].astype(F32)
            first = ((gain[s : s + 1] * start + back) * (0.5 * live)).astype(BF16)
            t_ref[slot] = first
            value = lax.dot_general(first, b_ref[slot], NT, preferred_element_type=F32)
            sums[slot + 1] = value + sums[links[slot]]

    coarse_sent(here, w_ref, *buffers, sems)
    gather(1 - here[3])
    coarse_round(here, u_view, lambda: gather(here[3]), kv, w_ref, *buffers, sems)
    coarse_sent(here, w_ref, *buffers, sems)


def final_body(links, v_ref, e_ref, b_ref, w_ref, t_ref, o_hbm, o_ref, o_sem):
    slots = b_ref.shape[0]
    points, count = slots + 64, 2 * slots + 64

    def chunk(i):
        rows = pl.ds(i * FINAL, FINAL)
        return pltpu.make_async_copy(o_ref.at[rows], o_hbm.at[rows], o_sem.at[i])

    @pl.loop(0, slots // FINAL)
    def _(i):
        gain = e_ref[pl.ds(pl.multiple_of(i * FINAL, 8), FINAL)] - 2.0
        for s in range(FINAL):
            slot = i * FINAL + s
            live = (slot < links[count]).astype(F32)
            back = back_of(links, points + slot, w_ref, b_ref[slot])
            second = gain[s : s + 1] * t_ref[slot].astype(F32) + (back - v_ref[slot].astype(F32)) * live
            o_ref[slot] = second.astype(BF16)
        chunk(i).start()

    for i in range(slots // FINAL):
        chunk(i).wait()


def local(vectors, energies, blocks, kernel, slot_coarse_kpoint, counts):
    v = vectors.transpose(0, 2, 1)
    slots = v.shape[0]
    chunks = slots // STEP
    rows = 2 * slots + 65
    query = lax.broadcasted_iota(jnp.int32, (rows, slots), 0)
    order = lax.broadcasted_iota(jnp.int32, (rows, slots), 1)
    point = jnp.pad(slot_coarse_kpoint, (0, rows - slots))[:, None] + jnp.maximum(query - slots, 0)
    match = (point == slot_coarse_kpoint[None, :]) & (order < query)
    plain = jnp.where(query == rows - 1, counts[0], jnp.where(order == query - (slots + 64), slot_coarse_kpoint[None, :], 0))
    links = jnp.max(jnp.where(query < slots + 64, jnp.where(match, order + 1, 0), plain), axis=1)
    coarse_shape = jax.ShapeDtypeStruct((4, 4, 4, 2, 8, 8, 128), BF16)
    fine_shape = jax.ShapeDtypeStruct(v.shape, BF16)
    block_shape = jax.ShapeDtypeStruct(blocks.shape, BF16)
    smem, vmem, hbm = (pl.BlockSpec(memory_space=m) for m in (pltpu.SMEM, pltpu.VMEM, pltpu.HBM))
    dma = pltpu.SemaphoreType.DMA
    t, held, w = pl.pallas_call(
        main_body,
        name="main",
        out_shape=(fine_shape, block_shape, coarse_shape),
        in_specs=[smem] + [hbm] * 4,
        out_specs=(vmem, vmem, vmem),
        scratch_shapes=[
            pltpu.VMEM(v.shape, BF16),
            pltpu.VMEM(energies.shape, F32),
            pltpu.VMEM(kernel.shape, BF16),
            pltpu.VMEM((slots + 1, 64, 256), F32),
            pltpu.VMEM((64, 2, 8, 8, 128), BF16),
            dma((chunks,)), dma((chunks,)), dma, dma,
        ] + ROUND + SEMS,
        compiler_params=pltpu.CompilerParams(collective_id=0, has_side_effects=True, vmem_limit_bytes=MAIN_VMEM),
    )(links, *(pltpu.with_memory_space_constraint(a, pltpu.HBM) for a in (v, energies, blocks, kernel)))
    out = pl.pallas_call(
        final_body,
        name="final",
        out_shape=fine_shape,
        in_specs=[smem] + [vmem] * 5,
        out_specs=hbm,
        scratch_shapes=[pltpu.VMEM(v.shape, BF16), dma((slots // FINAL,))],
        compiler_params=pltpu.CompilerParams(vmem_limit_bytes=FINAL_VMEM),
    )(links, v, energies, held, w.reshape(64, 2, 64, 128), t)
    return out.transpose(0, 2, 1)


def solution(mesh):
    both = ("row", "col")
    in_specs = (P(both, None, None), P(both, None), P(both, None, None), P("row", "col"), P(both), P(both))
    return jax.shard_map(local, mesh=mesh, in_specs=in_specs, out_specs=P(both, None, None), check_vma=False)
```

```python
import functools

import jax
import jax.numpy as jnp
from jax import lax
from jax.experimental import pallas as pl
from jax.experimental.pallas import tpu as pltpu
from jax.sharding import PartitionSpec as P

MESH = pl.DeviceIdType.MESH
F32 = jnp.float32
BF16 = jnp.bfloat16
STEP, MIDDLE, FINAL = 16, 48, 32
MAIN_VMEM = 22 << 20
FINAL_VMEM = 8 << 20
X, Y, Z = 0, 1, 2
GROUPS = ((slice(0, 3), X, Y, Z), (slice(3, 6), Y, Z, X), (slice(6, 8), Z, X, Y))
FAR, NEAR = (2, 1, 3, 0), (0, 1, 3, 2)
STEPS = [(i, j) for i in NEAR for j in NEAR][1:]
NT = (((1,), (1,)), ((), ()))


def position():
    r, c = lax.axis_index("row"), lax.axis_index("col")
    return (lax.div(c, 2), lax.div(r, 4), lax.rem(r, 4), lax.rem(c, 2))


def moved(here, moves):
    there = list(here)
    for dim, step in moves:
        there[dim] = 1 - there[dim] if dim == 3 else lax.rem(there[dim] + step, 4)
    return there


def device(here, moves):
    x, y, z, k = moved(here, moves)
    return (y * 4 + z, x * 2 + k)


def natural(fixed):
    return tuple(fixed.get(d, slice(None)) for d in range(3))


SIBLING = (3, 1)
XK = [((X, i),) * (i > 0) + (SIBLING,) * q for i in range(4) for q in range(2)][1:]
PEERS = [((d, o),) for d in range(3) for o in (1, 2, 3)]
PEERS += [((a, i), (b, j)) for a, b in ((X, Y), (Y, Z), (Z, X)) for i in (1, 2, 3) for j in (1, 2, 3)]
PEERS += [(SIBLING,)] + [((X, o), SIBLING) for o in (1, 2, 3)]


def greet(here):
    barrier = pltpu.get_barrier_semaphore()
    for moves in PEERS:
        pl.semaphore_signal(barrier, inc=1, device_id=device(here, moves), device_id_type=MESH)


def greeted():
    pl.semaphore_wait(pltpu.get_barrier_semaphore(), len(PEERS))


def send(here, src, dst, ss, rs, moves):
    pltpu.make_async_remote_copy(src_ref=src, dst_ref=dst, send_sem=ss, recv_sem=rs, device_id=device(here, moves), device_id_type=MESH).start()


def landed(here, ref, rs):
    pltpu.make_async_remote_copy(src_ref=ref, dst_ref=ref, send_sem=rs, recv_sem=rs, device_id=device(here, (SIBLING,)), device_id_type=MESH).wait_recv()


def gone(here, ref, ss):
    pltpu.make_async_remote_copy(src_ref=ref, dst_ref=ref, send_sem=ss, recv_sem=ss, device_id=device(here, (SIBLING,)), device_id_type=MESH).wait_send()


def moves_of(*pairs):
    return tuple(p for p in pairs if p[1])


def coarse_round(here, u_ref, own_half, kv, w_ref, core_in, s1, r1, s2, r2, ub, ul, prod, pw, rw, sems):
    (core_ss, core_rs, big_ss, big_rs, pl_ss, pl_rs, yz_ss, yz_rs, pr_ss, pr_rs, ap_ss, ap_rs, ab_ss, ab_rs, fin_ss, fin_rs) = sems
    x, y, z, k = here
    along = [[moved(here, ((d, o),))[d] for o in range(4)] for d in range(3)]

    for r in FAR:
        for g, (v, c, a, b) in enumerate(GROUPS):
            ix = natural({a: along[a][r]})
            send(here, u_ref.at[ix[0], 1 - k, ix[1], ix[2], v], core_in.at[ix + (v,)], core_ss, core_rs.at[g, r], (SIBLING,))
    own_half()
    for r in FAR:
        for g, (v, c, a, b) in enumerate(GROUPS):
            ix = natural({a: along[a][r]})
            landed(here, core_in.at[ix + (v,)], core_rs.at[g, r])
            s1[ix + (v,)] = (u_ref[ix[0], k, ix[1], ix[2], v].astype(F32) + core_in[ix + (v,)].astype(F32)).astype(BF16)
            for o in (2, 1, 3):
                src = s1.at[natural({a: along[a][r], c: along[c][o]}) + (v,)]
                send(here, src, r1.at[o - 1, along[a][r], :, v], big_ss, big_rs.at[g, r], ((c, o),))
    for r in FAR:
        for g, (v, c, a, b) in enumerate(GROUPS):
            row = along[a][r]
            landed(here, r1.at[:, row, :, v], big_rs.at[g, r])
            total = s1[natural({a: row, c: here[c]}) + (v,)].astype(F32)
            for o in range(3):
                total = total + r1[o, row, :, v].astype(F32)
            s2[row, :, v] = total.astype(BF16)
            for j in FAR:
                if (r, j) != (0, 0):
                    send(here, s2.at[row, along[b][j], v], r2.at[STEPS.index((r, j)), v], pl_ss, pl_rs.at[g], moves_of((a, r), (b, j)))
    for g, (v, c, a, b) in enumerate(GROUPS):
        landed(here, r2.at[:, v], pl_rs.at[g])
        total = s2[here[a], here[b], v].astype(F32)
        for i in range(15):
            total = total + r2[i, v].astype(F32)
        ub[y, z, v] = total.astype(BF16)
    for p, q in STEPS:
        send(here, ub.at[y, z], ub.at[y, z], yz_ss, yz_rs.at[p], moves_of((Y, p), (Z, q)))
    for first, r in enumerate(NEAR):
        row = along[Y][r]
        landed(here, ub.at[row] if r else ub.at[row, pl.ds(0, 3)], yz_rs.at[(-r) % 4])
        for q in range(4):
            ul[:, q * 128 : q * 128 + 128] = ub[row, q].reshape(64, 128)
        for o in FAR:
            n = along[X][o]
            rows = pl.ds(pl.multiple_of(n * 256, 256), 256)
            part = lax.dot_general(ul[...], kv[rows, pl.ds(pl.multiple_of(row * 512, 512), 512)], NT, preferred_element_type=F32)
            part = part if first == 0 else prod[o] + part
            if first < 3:
                prod[o] = part
                continue
            for h in range(2):
                pw[n, h] = part[:, h * 128 : h * 128 + 128].astype(BF16).reshape(8, 8, 128)
            for i, moves in enumerate(XK):
                if dict(moves).get(X, 0) == o:
                    there = moved(here, moves)
                    send(here, pw.at[there[0], there[3]], rw.at[i], pr_ss, pr_rs, moves)
    landed(here, rw, pr_rs)
    total = pw[x, k].astype(F32)
    for i in range(7):
        total = total + rw[i].astype(F32)
    w_ref[y, z, x, k] = total.astype(BF16)

    def part_of(v, fixed):
        ix = natural(fixed)
        return w_ref.at[ix[1], ix[2], ix[0], k, v]

    for p, q in STEPS:
        for g, (v, c, a, b) in enumerate(GROUPS):
            block = part_of(v, {d: here[d] for d in range(3)})
            send(here, block, block, ap_ss, ap_rs.at[g, p], moves_of((a, p), (b, q)))
    some = pl.ds(0, 3)
    for r in NEAR:
        for g, (v, c, a, b) in enumerate(GROUPS):
            row = {a: along[a][r], c: here[c]}
            landed(here, part_of(v, row if r else row | {b: some}), ap_rs.at[g, (-r) % 4])
            block = part_of(v, row)
            for o in (2, 1, 3):
                send(here, block, block, ab_ss, ab_rs.at[g, r, o - 1], ((c, o),))
            send(here, block, block, fin_ss, fin_rs, (SIBLING,))
    for r in NEAR:
        for g, (v, c, a, b) in enumerate(GROUPS):
            for o in (1, 3, 2):
                block = part_of(v, {a: along[a][r], c: along[c][4 - o]})
                landed(here, block, ab_rs.at[g, r, o - 1])
                send(here, block, block, fin_ss, fin_rs, (SIBLING,))
    landed(here, w_ref.at[:, :, :, 1 - k], fin_rs)


def coarse_sent(here, w_ref, core_in, s1, r1, s2, r2, ub, ul, prod, pw, rw, sems):
    core_ss, big_ss, pl_ss, yz_ss, pr_ss, ap_ss, ab_ss, fin_ss = sems[::2]
    some = pl.ds(0, 3)
    gone(here, core_in, core_ss)
    gone(here, s1.at[some], big_ss)
    gone(here, r2, pl_ss)
    gone(here, r2, yz_ss)
    gone(here, rw, pr_ss)
    gone(here, r2, ap_ss)
    gone(here, w_ref.at[some, :, :, 0], ab_ss)
    gone(here, w_ref.at[:, :, :, 0], fin_ss)


ROUND = [
    pltpu.VMEM((4, 4, 4, 8, 8, 128), BF16),
    pltpu.VMEM((4, 4, 4, 8, 8, 128), BF16),
    pltpu.VMEM((3, 4, 4, 8, 8, 128), BF16),
    pltpu.VMEM((4, 4, 8, 8, 128), BF16),
    pltpu.VMEM((15, 8, 8, 128), BF16),
    pltpu.VMEM((4, 4, 8, 8, 128), BF16),
    pltpu.VMEM((64, 512), BF16),
    pltpu.VMEM((4, 64, 256), F32),
    pltpu.VMEM((4, 2, 8, 8, 128), BF16),
    pltpu.VMEM((7, 8, 8, 128), BF16),
]
SEMS = [pltpu.SemaphoreType.DMA(s) for n in ((3, 4), (3, 4), (3,), (4,), (), (3, 4), (3, 4, 3), ()) for s in ((), n)]


def back_of(points, slot, w_ref, b):
    p = points[slot]
    w = jnp.concatenate([w_ref[p, 0], w_ref[p, 1]], axis=1)
    return jnp.dot(w, b, preferred_element_type=F32)


def main_body(links, v_hbm, e_hbm, b_hbm, k_hbm, t_ref, b_ref, w_ref,
              v_ref, e_ref, kv, sums, u_ref, v_sem, b_sem, e_sem, k_sem, *scratch):
    here = position()
    slots = b_ref.shape[0]
    chunks = slots // STEP
    greet(here)

    def chunk(i):
        rows = pl.ds(i * STEP, STEP)
        return (
            pltpu.make_async_copy(v_hbm.at[rows], v_ref.at[rows], v_sem.at[i]),
            pltpu.make_async_copy(b_hbm.at[rows], b_ref.at[rows], b_sem.at[i]),
        )

    for i in range(chunks):
        for copy in chunk(i):
            copy.start()
    energies = pltpu.make_async_copy(e_hbm, e_ref, e_sem)
    energies.start()
    table = pltpu.make_async_copy(k_hbm, kv, k_sem)
    table.start()
    sums[0] = jnp.zeros(sums.shape[1:], F32)

    points, count = slots + 64, 2 * slots + 64

    def gather(half):
        @pl.loop(0, 32, unroll=8)
        def _(i):
            p = lax.div(i, 8) * 16 + half * 8 + lax.rem(i, 8)
            value = sums[links[slots + p]].astype(BF16)
            u_ref[p, 0] = value[:, :128].reshape(8, 8, 128)
            u_ref[p, 1] = value[:, 128:].reshape(8, 8, 128)

    @pl.loop(0, chunks)
    def _(i):
        for copy in chunk(i):
            copy.wait()
        for s in range(STEP):
            slot = i * STEP + s
            live = (slot < links[count]).astype(BF16)
            value = lax.dot_general(v_ref[slot] * live, b_ref[slot], NT, preferred_element_type=F32)
            sums[slot + 1] = value + sums[links[slot]]

    gather(1 - here[3])
    energies.wait()
    table.wait()
    greeted()
    u_view = u_ref.reshape(4, 2, 4, 4, 8, 8, 128)
    buffers, sems = scratch[: len(ROUND)], scratch[len(ROUND) :]
    coarse_round(here, u_view, lambda: gather(here[3]), kv, w_ref, *buffers, sems)
    w_view = w_ref.reshape(64, 2, 64, 128)

    @pl.loop(0, slots // MIDDLE)
    def _(i):
        gain = e_ref[pl.ds(pl.multiple_of(i * MIDDLE, 8), MIDDLE)] - 2.0
        for s in range(MIDDLE):
            slot = i * MIDDLE + s
            live = (slot < links[count]).astype(F32)
            back = back_of(links, points + slot, w_view, b_ref[slot])
            start = v_ref[slot].astype(F32)
            first = ((gain[s : s + 1] * start + back) * (0.5 * live)).astype(BF16)
            t_ref[slot] = first
            value = lax.dot_general(first, b_ref[slot], NT, preferred_element_type=F32)
            sums[slot + 1] = value + sums[links[slot]]

    coarse_sent(here, w_ref, *buffers, sems)
    gather(1 - here[3])
    coarse_round(here, u_view, lambda: gather(here[3]), kv, w_ref, *buffers, sems)
    coarse_sent(here, w_ref, *buffers, sems)


def final_body(links, v_ref, e_ref, b_ref, w_ref, t_ref, o_hbm, o_ref, o_sem):
    slots = b_ref.shape[0]
    points, count = slots + 64, 2 * slots + 64

    def chunk(i):
        rows = pl.ds(i * FINAL, FINAL)
        return pltpu.make_async_copy(o_ref.at[rows], o_hbm.at[rows], o_sem.at[i])

    @pl.loop(0, slots // FINAL)
    def _(i):
        gain = e_ref[pl.ds(pl.multiple_of(i * FINAL, 8), FINAL)] - 2.0
        for s in range(FINAL):
            slot = i * FINAL + s
            live = (slot < links[count]).astype(F32)
            back = back_of(links, points + slot, w_ref, b_ref[slot])
            second = gain[s : s + 1] * t_ref[slot].astype(F32) + (back - v_ref[slot].astype(F32)) * live
            o_ref[slot] = second.astype(BF16)
        chunk(i).start()

    for i in range(slots // FINAL):
        chunk(i).wait()


def local(vectors, energies, blocks, kernel, slot_coarse_kpoint, counts):
    v = vectors.transpose(0, 2, 1)
    slots = v.shape[0]
    chunks = slots // STEP
    rows = 2 * slots + 65
    query = lax.broadcasted_iota(jnp.int32, (rows, slots), 0)
    order = lax.broadcasted_iota(jnp.int32, (rows, slots), 1)
    point = jnp.pad(slot_coarse_kpoint, (0, rows - slots))[:, None] + jnp.maximum(query - slots, 0)
    match = (point == slot_coarse_kpoint[None, :]) & (order < query)
    plain = jnp.where(query == rows - 1, counts[0], jnp.where(order == query - (slots + 64), slot_coarse_kpoint[None, :], 0))
    links = jnp.max(jnp.where(query < slots + 64, jnp.where(match, order + 1, 0), plain), axis=1)
    coarse_shape = jax.ShapeDtypeStruct((4, 4, 4, 2, 8, 8, 128), BF16)
    fine_shape = jax.ShapeDtypeStruct(v.shape, BF16)
    block_shape = jax.ShapeDtypeStruct(blocks.shape, BF16)
    smem, vmem, hbm = (pl.BlockSpec(memory_space=m) for m in (pltpu.SMEM, pltpu.VMEM, pltpu.HBM))
    dma = pltpu.SemaphoreType.DMA
    t, held, w = pl.pallas_call(
        main_body,
        name="main",
        out_shape=(fine_shape, block_shape, coarse_shape),
        in_specs=[smem] + [hbm] * 4,
        out_specs=(vmem, vmem, vmem),
        scratch_shapes=[
            pltpu.VMEM(v.shape, BF16),
            pltpu.VMEM(energies.shape, F32),
            pltpu.VMEM(kernel.shape, BF16),
            pltpu.VMEM((slots + 1, 64, 256), F32),
            pltpu.VMEM((64, 2, 8, 8, 128), BF16),
            dma((chunks,)), dma((chunks,)), dma, dma,
        ] + ROUND + SEMS,
        compiler_params=pltpu.CompilerParams(collective_id=0, has_side_effects=True, vmem_limit_bytes=MAIN_VMEM),
    )(links, *(pltpu.with_memory_space_constraint(a, pltpu.HBM) for a in (v, energies, blocks, kernel)))
    out = pl.pallas_call(
        final_body,
        name="final",
        out_shape=fine_shape,
        in_specs=[smem] + [vmem] * 5,
        out_specs=hbm,
        scratch_shapes=[pltpu.VMEM(v.shape, BF16), dma((slots // FINAL,))],
        compiler_params=pltpu.CompilerParams(vmem_limit_bytes=FINAL_VMEM),
    )(links, v, energies, held, w.reshape(64, 2, 64, 128), t)
    return out.transpose(0, 2, 1)


def solution(mesh):
    both = ("row", "col")
    in_specs = (P(both, None, None), P(both, None), P(both, None, None), P("row", "col"), P(both), P(both))
    return jax.shard_map(local, mesh=mesh, in_specs=in_specs, out_specs=P(both, None, None), check_vma=False)
```

```python
import functools

import jax
import jax.numpy as jnp
from jax import lax
from jax.experimental import pallas as pl
from jax.experimental.pallas import tpu as pltpu
from jax.sharding import PartitionSpec as P

MESH = pl.DeviceIdType.MESH
F32 = jnp.float32
BF16 = jnp.bfloat16
STEP, MIDDLE, FINAL = 16, 48, 32
MAIN_VMEM = 22 << 20
FINAL_VMEM = 8 << 20
X, Y, Z = 0, 1, 2
GROUPS = ((slice(0, 3), X, Y, Z), (slice(3, 6), Y, Z, X), (slice(6, 8), Z, X, Y))
FAR, NEAR = (2, 1, 3, 0), (0, 1, 3, 2)
STEPS = [(i, j) for i in NEAR for j in NEAR][1:]
NT = (((1,), (1,)), ((), ()))


def position():
    r, c = lax.axis_index("row"), lax.axis_index("col")
    return (lax.div(c, 2), lax.div(r, 4), lax.rem(r, 4), lax.rem(c, 2))


def moved(here, moves):
    there = list(here)
    for dim, step in moves:
        there[dim] = 1 - there[dim] if dim == 3 else lax.rem(there[dim] + step, 4)
    return there


def device(here, moves):
    x, y, z, k = moved(here, moves)
    return (y * 4 + z, x * 2 + k)


def natural(fixed):
    return tuple(fixed.get(d, slice(None)) for d in range(3))


SIBLING = (3, 1)
XK = [((X, i),) * (i > 0) + (SIBLING,) * q for i in range(4) for q in range(2)][1:]
PEERS = [((d, o),) for d in range(3) for o in (1, 2, 3)]
PEERS += [((a, i), (b, j)) for a, b in ((X, Y), (Y, Z), (Z, X)) for i in (1, 2, 3) for j in (1, 2, 3)]
PEERS += [(SIBLING,)] + [((X, o), SIBLING) for o in (1, 2, 3)]


def greet(here):
    barrier = pltpu.get_barrier_semaphore()
    for moves in PEERS:
        pl.semaphore_signal(barrier, inc=1, device_id=device(here, moves), device_id_type=MESH)


def greeted():
    pl.semaphore_wait(pltpu.get_barrier_semaphore(), len(PEERS))


def send(here, src, dst, ss, rs, moves):
    pltpu.make_async_remote_copy(src_ref=src, dst_ref=dst, send_sem=ss, recv_sem=rs, device_id=device(here, moves), device_id_type=MESH).start()


def landed(here, ref, rs):
    pltpu.make_async_remote_copy(src_ref=ref, dst_ref=ref, send_sem=rs, recv_sem=rs, device_id=device(here, (SIBLING,)), device_id_type=MESH).wait_recv()


def gone(here, ref, ss):
    pltpu.make_async_remote_copy(src_ref=ref, dst_ref=ref, send_sem=ss, recv_sem=ss, device_id=device(here, (SIBLING,)), device_id_type=MESH).wait_send()


def moves_of(*pairs):
    return tuple(p for p in pairs if p[1])


def coarse_round(here, u_ref, own_half, kv, w_ref, core_in, s1, r1, s2, r2, ub, ul, prod, pw, rw, sems):
    (core_ss, core_rs, big_ss, big_rs, pl_ss, pl_rs, yz_ss, yz_rs, pr_ss, pr_rs, ap_ss, ap_rs, ab_ss, ab_rs, fin_ss, fin_rs) = sems
    x, y, z, k = here
    along = [[moved(here, ((d, o),))[d] for o in range(4)] for d in range(3)]

    for r in FAR:
        for g, (v, c, a, b) in enumerate(GROUPS):
            ix = natural({a: along[a][r]})
            send(here, u_ref.at[ix[0], 1 - k, ix[1], ix[2], v], core_in.at[ix + (v,)], core_ss, core_rs.at[g, r], (SIBLING,))
    own_half()
    for r in FAR:
        for g, (v, c, a, b) in enumerate(GROUPS):
            ix = natural({a: along[a][r]})
            landed(here, core_in.at[ix + (v,)], core_rs.at[g, r])
            s1[ix + (v,)] = (u_ref[ix[0], k, ix[1], ix[2], v].astype(F32) + core_in[ix + (v,)].astype(F32)).astype(BF16)
            for o in (2, 1, 3):
                src = s1.at[natural({a: along[a][r], c: along[c][o]}) + (v,)]
                send(here, src, r1.at[o - 1, along[a][r], :, v], big_ss, big_rs.at[g, r], ((c, o),))
    for r in FAR:
        for g, (v, c, a, b) in enumerate(GROUPS):
            row = along[a][r]
            landed(here, r1.at[:, row, :, v], big_rs.at[g, r])
            total = s1[natural({a: row, c: here[c]}) + (v,)].astype(F32)
            for o in range(3):
                total = total + r1[o, row, :, v].astype(F32)
            s2[row, :, v] = total.astype(BF16)
            for j in FAR:
                if (r, j) != (0, 0):
                    send(here, s2.at[row, along[b][j], v], r2.at[STEPS.index((r, j)), v], pl_ss, pl_rs.at[g], moves_of((a, r), (b, j)))
    for g, (v, c, a, b) in enumerate(GROUPS):
        landed(here, r2.at[:, v], pl_rs.at[g])
        total = s2[here[a], here[b], v].astype(F32)
        for i in range(15):
            total = total + r2[i, v].astype(F32)
        ub[y, z, v] = total.astype(BF16)
    for p, q in STEPS:
        send(here, ub.at[y, z], ub.at[y, z], yz_ss, yz_rs.at[p], moves_of((Y, p), (Z, q)))
    for first, r in enumerate(NEAR):
        row = along[Y][r]
        landed(here, ub.at[row] if r else ub.at[row, pl.ds(0, 3)], yz_rs.at[(-r) % 4])
        for q in range(4):
            ul[:, q * 128 : q * 128 + 128] = ub[row, q].reshape(64, 128)
        for o in FAR:
            n = along[X][o]
            rows = pl.ds(pl.multiple_of(n * 256, 256), 256)
            part = lax.dot_general(ul[...], kv[rows, pl.ds(pl.multiple_of(row * 512, 512), 512)], NT, preferred_element_type=F32)
            part = part if first == 0 else prod[o] + part
            if first < 3:
                prod[o] = part
                continue
            for h in range(2):
                pw[n, h] = part[:, h * 128 : h * 128 + 128].astype(BF16).reshape(8, 8, 128)
            for i, moves in enumerate(XK):
                if dict(moves).get(X, 0) == o:
                    there = moved(here, moves)
                    send(here, pw.at[there[0], there[3]], rw.at[i], pr_ss, pr_rs, moves)
    landed(here, rw, pr_rs)
    total = pw[x, k].astype(F32)
    for i in range(7):
        total = total + rw[i].astype(F32)
    w_ref[y, z, x, k] = total.astype(BF16)

    def part_of(v, fixed):
        ix = natural(fixed)
        return w_ref.at[ix[1], ix[2], ix[0], k, v]

    for p, q in STEPS:
        for g, (v, c, a, b) in enumerate(GROUPS):
            block = part_of(v, {d: here[d] for d in range(3)})
            send(here, block, block, ap_ss, ap_rs.at[g, p], moves_of((a, p), (b, q)))
    some = pl.ds(0, 3)
    for r in NEAR:
        for g, (v, c, a, b) in enumerate(GROUPS):
            row = {a: along[a][r], c: here[c]}
            landed(here, part_of(v, row if r else row | {b: some}), ap_rs.at[g, (-r) % 4])
            block = part_of(v, row)
            for o in (2, 1, 3):
                send(here, block, block, ab_ss, ab_rs.at[g, r, o - 1], ((c, o),))
            send(here, block, block, fin_ss, fin_rs, (SIBLING,))
    for r in NEAR:
        for g, (v, c, a, b) in enumerate(GROUPS):
            for o in (1, 3, 2):
                block = part_of(v, {a: along[a][r], c: along[c][4 - o]})
                landed(here, block, ab_rs.at[g, r, o - 1])
                send(here, block, block, fin_ss, fin_rs, (SIBLING,))
    landed(here, w_ref.at[:, :, :, 1 - k], fin_rs)


def coarse_sent(here, w_ref, core_in, s1, r1, s2, r2, ub, ul, prod, pw, rw, sems):
    core_ss, big_ss, pl_ss, yz_ss, pr_ss, ap_ss, ab_ss, fin_ss = sems[::2]
    some = pl.ds(0, 3)
    gone(here, core_in, core_ss)
    gone(here, s1.at[some], big_ss)
    gone(here, r2, pl_ss)
    gone(here, r2, yz_ss)
    gone(here, rw, pr_ss)
    gone(here, r2, ap_ss)
    gone(here, w_ref.at[some, :, :, 0], ab_ss)
    gone(here, w_ref.at[:, :, :, 0], fin_ss)


ROUND = [
    pltpu.VMEM((4, 4, 4, 8, 8, 128), BF16),
    pltpu.VMEM((4, 4, 4, 8, 8, 128), BF16),
    pltpu.VMEM((3, 4, 4, 8, 8, 128), BF16),
    pltpu.VMEM((4, 4, 8, 8, 128), BF16),
    pltpu.VMEM((15, 8, 8, 128), BF16),
    pltpu.VMEM((4, 4, 8, 8, 128), BF16),
    pltpu.VMEM((64, 512), BF16),
    pltpu.VMEM((4, 64, 256), F32),
    pltpu.VMEM((4, 2, 8, 8, 128), BF16),
    pltpu.VMEM((7, 8, 8, 128), BF16),
]
SEMS = [pltpu.SemaphoreType.DMA(s) for n in ((3, 4), (3, 4), (3,), (4,), (), (3, 4), (3, 4, 3), ()) for s in ((), n)]


def back_of(links, slot, w_ref, b):
    p = links[2, slot]
    w = jnp.concatenate([w_ref[p, 0], w_ref[p, 1]], axis=1)
    return jnp.dot(w, b, preferred_element_type=F32)


def main_body(links, v_hbm, e_hbm, b_hbm, k_hbm, t_ref, b_ref, w_ref,
              v_ref, e_ref, kv, sums, u_ref, v_sem, b_sem, e_sem, k_sem, *scratch):
    here = position()
    slots = b_ref.shape[0]
    chunks = slots // STEP
    greet(here)

    def chunk(i):
        rows = pl.ds(i * STEP, STEP)
        return (
            pltpu.make_async_copy(v_hbm.at[rows], v_ref.at[rows], v_sem.at[i]),
            pltpu.make_async_copy(b_hbm.at[rows], b_ref.at[rows], b_sem.at[i]),
        )

    for i in range(chunks):
        for copy in chunk(i):
            copy.start()
    energies = pltpu.make_async_copy(e_hbm, e_ref, e_sem)
    energies.start()
    table = pltpu.make_async_copy(k_hbm, kv, k_sem)
    table.start()
    sums[0] = jnp.zeros(sums.shape[1:], F32)


    def gather(half):
        @pl.loop(0, 32, unroll=8)
        def _(i):
            p = lax.div(i, 8) * 16 + half * 8 + lax.rem(i, 8)
            value = sums[links[1, p]].astype(BF16)
            u_ref[p, 0] = value[:, :128].reshape(8, 8, 128)
            u_ref[p, 1] = value[:, 128:].reshape(8, 8, 128)

    @pl.loop(0, chunks)
    def _(i):
        for copy in chunk(i):
            copy.wait()
        for s in range(STEP):
            slot = i * STEP + s
            live = (slot < links[1, 64]).astype(BF16)
            value = lax.dot_general(v_ref[slot] * live, b_ref[slot], NT, preferred_element_type=F32)
            sums[slot + 1] = value + sums[links[0, slot]]

    gather(1 - here[3])
    energies.wait()
    table.wait()
    greeted()
    u_view = u_ref.reshape(4, 2, 4, 4, 8, 8, 128)
    buffers, sems = scratch[: len(ROUND)], scratch[len(ROUND) :]
    coarse_round(here, u_view, lambda: gather(here[3]), kv, w_ref, *buffers, sems)
    w_view = w_ref.reshape(64, 2, 64, 128)

    @pl.loop(0, slots // MIDDLE)
    def _(i):
        gain = e_ref[pl.ds(pl.multiple_of(i * MIDDLE, 8), MIDDLE)] - 2.0
        for s in range(MIDDLE):
            slot = i * MIDDLE + s
            live = (slot < links[1, 64]).astype(F32)
            back = back_of(links, slot, w_view, b_ref[slot])
            start = v_ref[slot].astype(F32)
            first = ((gain[s : s + 1] * start + back) * (0.5 * live)).astype(BF16)
            t_ref[slot] = first
            value = lax.dot_general(first, b_ref[slot], NT, preferred_element_type=F32)
            sums[slot + 1] = value + sums[links[0, slot]]

    coarse_sent(here, w_ref, *buffers, sems)
    gather(1 - here[3])
    coarse_round(here, u_view, lambda: gather(here[3]), kv, w_ref, *buffers, sems)
    coarse_sent(here, w_ref, *buffers, sems)


def final_body(links, v_ref, e_ref, b_ref, w_ref, t_ref, o_hbm, o_ref, o_sem):
    slots = b_ref.shape[0]

    def chunk(i):
        rows = pl.ds(i * FINAL, FINAL)
        return pltpu.make_async_copy(o_ref.at[rows], o_hbm.at[rows], o_sem.at[i])

    @pl.loop(0, slots // FINAL)
    def _(i):
        gain = e_ref[pl.ds(pl.multiple_of(i * FINAL, 8), FINAL)] - 2.0
        for s in range(FINAL):
            slot = i * FINAL + s
            live = (slot < links[1, 64]).astype(F32)
            back = back_of(links, slot, w_ref, b_ref[slot])
            second = gain[s : s + 1] * t_ref[slot].astype(F32) + (back - v_ref[slot].astype(F32)) * live
            o_ref[slot] = second.astype(BF16)
        chunk(i).start()

    for i in range(slots // FINAL):
        chunk(i).wait()


def local(vectors, energies, blocks, kernel, slot_coarse_kpoint, counts):
    v = vectors.transpose(0, 2, 1)
    slots = v.shape[0]
    chunks = slots // STEP
    kind, query, order = (lax.broadcasted_iota(jnp.int32, (3, slots, slots), d) for d in range(3))
    here, there = slot_coarse_kpoint[None, :, None], slot_coarse_kpoint[None, None, :]
    match = (jnp.where(kind == 0, here, query) == there) & ((order < query) | (kind == 1))
    found = jnp.where(match, order + 1, 0)
    found = jnp.where((kind == 1) & (query == 64), counts[0], found)
    links = jnp.max(jnp.where(kind == 2, here, found), axis=2)
    coarse_shape = jax.ShapeDtypeStruct((4, 4, 4, 2, 8, 8, 128), BF16)
    fine_shape = jax.ShapeDtypeStruct(v.shape, BF16)
    block_shape = jax.ShapeDtypeStruct(blocks.shape, BF16)
    smem, vmem, hbm = (pl.BlockSpec(memory_space=m) for m in (pltpu.SMEM, pltpu.VMEM, pltpu.HBM))
    dma = pltpu.SemaphoreType.DMA
    t, held, w = pl.pallas_call(
        main_body,
        name="main",
        out_shape=(fine_shape, block_shape, coarse_shape),
        in_specs=[smem] + [hbm] * 4,
        out_specs=(vmem, vmem, vmem),
        scratch_shapes=[
            pltpu.VMEM(v.shape, BF16),
            pltpu.VMEM(energies.shape, F32),
            pltpu.VMEM(kernel.shape, BF16),
            pltpu.VMEM((slots + 1, 64, 256), F32),
            pltpu.VMEM((64, 2, 8, 8, 128), BF16),
            dma((chunks,)), dma((chunks,)), dma, dma,
        ] + ROUND + SEMS,
        compiler_params=pltpu.CompilerParams(collective_id=0, has_side_effects=True, vmem_limit_bytes=MAIN_VMEM),
    )(links, *(pltpu.with_memory_space_constraint(a, pltpu.HBM) for a in (v, energies, blocks, kernel)))
    out = pl.pallas_call(
        final_body,
        name="final",
        out_shape=fine_shape,
        in_specs=[smem] + [vmem] * 5,
        out_specs=hbm,
        scratch_shapes=[pltpu.VMEM(v.shape, BF16), dma((slots // FINAL,))],
        compiler_params=pltpu.CompilerParams(vmem_limit_bytes=FINAL_VMEM),
    )(links, v, energies, held, w.reshape(64, 2, 64, 128), t)
    return out.transpose(0, 2, 1)


def solution(mesh):
    both = ("row", "col")
    in_specs = (P(both, None, None), P(both, None), P(both, None, None), P("row", "col"), P(both), P(both))
    return jax.shard_map(local, mesh=mesh, in_specs=in_specs, out_specs=P(both, None, None), check_vma=False)
```
